32 devices in a mesh: tok: 16 (over z, x, core), lyr: 2 (over y).
Axes of the slice: x: 2, y: 2, z: 4, core: 2. Of those that a mesh axis runs over, the one named last changes fastest.
Arguments:
- feature_codes: bfloat16 [4, 2048, 2, 256], P('lyr', 'tok'), may hold values from 0 to 21, as said below
- block_ids: int32 [4, 2048, 2], P('lyr', 'tok'), may hold values from 0 to 31, all different within a row; in each aligned block of 128 rows (0 to 127, 128 to 255, ..., all dimensions but the last counted through in order) at most 16 rows name the same one
- target_layer: int32 [2048], P('tok'), may hold values from 0 to 3
- request_ids: int32 [2048], P('tok'), may hold values from 0 to 15
- target_resid: bfloat16 [2048, 2304], P('tok'), may hold values from -6 to 6
- decoder: bfloat16 [4, 8192, 2304], P('lyr', 'tok'), may hold values from -0.25 to 0.25
Outputs:
- scores: bfloat16 [4, 2048, 2, 256], P('lyr', 'tok')
- request_totals: float32 [16, 4, 8192], P(None, 'lyr', 'tok')
The draws below stay inside these ranges and needn't reach their ends.
Inputs may be any that keep to these rules, and one draw needn't show every extreme that they name: `block_ids`: the 2 panel indices of one token at one source layer are distinct; among the 128 tokens of one index of tok at one source layer no panel is named by more than 16 of them, a bound that some block reaches. `feature_codes`: nonnegative, with many entries zero.
All inputs are finite; a program needn't handle non-finite values.
Results may differ from the reference program's by a relative error of at most 0.0053.
Values may be sent and summed in bfloat16 or wider, within the bound.
A program may use at most 64 MiB of HBM per device.

```python
import math
import jax
import jax.numpy as jnp
import numpy as np
from jax import lax

D = 2304
PANEL = 256
PANELS = 32
KACT = 2
REQUESTS = 16
TOK_DEV = 128
CAP = 16
F = 8192
LAYERS = 4
TOKENS = 2048
N_TOK = 16


def draw_feature_codes(key, part):
    normal_key, scale_key = jax.random.split(jax.random.fold_in(key, 17))
    normal_part = jax.random.normal(normal_key, (LAYERS, TOKENS, KACT, PANEL), jnp.float32)
    spread = jnp.exp(jax.random.uniform(scale_key, (LAYERS, TOKENS, KACT, 1), jnp.float32, jnp.log(0.5), jnp.log(2.0)))
    return (jnp.clip(normal_part, 0.0, 5.0) * spread).astype(jnp.bfloat16)


def touch_ends(array, rng, least, high):
    dims = array.shape
    spot = [jax.random.randint(jax.random.fold_in(rng, axis), (), 0, dims[axis]) for axis in range(len(dims))]
    array = array.at[tuple(spot)].set(least)
    longest = dims.index(max(dims))
    spot[longest] = (spot[longest] + 1) % dims[longest]
    return array.at[tuple(spot)].set(high)


def block_scale(key, dims, pieces, low, largest):
    level = 1.0
    for position, parts in pieces:
        draws = jax.random.uniform(jax.random.fold_in(jax.random.fold_in(key, 6), position), (parts,), jnp.float32, low / len(pieces), largest / len(pieces))
        level = level * jnp.repeat(jnp.exp(draws), dims[position] // parts).reshape((-1,) + (1,) * (len(dims) - 1 - position))
    return level


def shared_out(stream_key, own, number, rows, count, top, bound, slope):
    sequence = jax.random.permutation(stream_key, count)
    heavy_load, usual = shares(count, rows * top, bound, slope, True), shares(count, rows * top, bound, slope, False)
    places = jnp.arange(count)

    def named(sizes, turn):
        used = int((sizes > 0).sum())
        fixed = max(1, used // 4)
        passed = fixed + (places - fixed + turn * (used - fixed)) % max(1, count - fixed)
        return jnp.zeros((count,), jnp.int32).at[sequence[jnp.where(places < fixed, places, passed)]].set(jnp.asarray(sizes, jnp.int32))

    sizes = jnp.where(number % 4 == 0, named(heavy_load, number // 4), named(usual, number - number // 4 - 1))
    mixed = jax.random.permutation(jax.random.fold_in(own, 3), count)
    giver, sink = mixed[0:count // 2 * 2:2], mixed[1:count // 2 * 2:2]
    margin = jnp.minimum(sizes[giver] - 1, bound - sizes[sink]) // 2
    margin = jnp.where((giver == sequence[0]) | (sink == sequence[0]) | (sizes[sink] == 0), 0, jnp.maximum(margin, 0))
    passed = jax.random.randint(jax.random.fold_in(own, 4), (count // 2,), 0, 1 << 20) % (margin + 1)
    sizes = sizes.at[giver].add(-passed).at[sink].add(passed)
    items = jnp.searchsorted(jnp.cumsum(sizes), jnp.arange(rows * top), side="right").astype(jnp.int32)
    table = items.reshape(top, rows).T
    table = table[jax.random.permutation(jax.random.fold_in(own, 1), rows)]
    turn = jax.random.randint(jax.random.fold_in(own, 2), (rows, 1), 0, top)
    return jnp.take_along_axis(table, (jnp.arange(top)[None, :] + turn) % top, axis=1)


def shares(amount, total, limit, skew, full):
    loads = [(1 << 20) // math.isqrt(rank ** skew) + 1 for rank in range(1, amount + 1)]
    largest = limit if full else min(limit, max(-(-total // amount), total * loads[0] // sum(loads)))
    least = 1 if total - largest >= amount - 1 else 0
    holding, rest = [largest] + [least] * (amount - 1), total - largest - least * (amount - 1)
    while rest > 0:
        free = [i for i in range(1, amount) if holding[i] < largest] or [i for i in range(1, amount) if holding[i] < limit]
        whole, remaining = sum([loads[i] for i in free]), rest
        for i in free:
            extra = min(limit - holding[i], max(1, remaining * loads[i] // whole), rest)
            holding[i] = holding[i] + extra
            rest = rest - extra
    return np.array(holding)


def bell_draw(stream_key, dims, scale, most, pieces=(), held_as=jnp.bfloat16):
    drawn = jax.random.normal(stream_key, dims, jnp.float32) * scale
    if len(pieces) > 0:
        drawn = block_scale(stream_key, dims, pieces, -0.22, 0.18) * drawn
    return jnp.clip(drawn, min=-most, max=most).astype(held_as)


def setup_inputs(seed: int = 0) -> dict:
    arg_keys = jax.random.split(jax.random.key(seed), 7)
    feature_codes = draw_feature_codes(jax.random.fold_in(arg_keys[6], 71), 0)
    block_ids_keys = jax.random.split(jax.random.fold_in(arg_keys[1], 1), LAYERS * TOKENS // TOK_DEV)
    block_ids_turns = jax.random.permutation(jax.random.fold_in(arg_keys[1], 3), LAYERS * TOKENS // TOK_DEV)
    block_ids = jax.vmap(lambda own, number: shared_out(jax.random.fold_in(arg_keys[1], 2), own, number, TOK_DEV, PANELS, KACT, CAP, 1))(block_ids_keys, block_ids_turns).reshape((LAYERS, TOKENS, KACT))
    target_layer = touch_ends(jax.random.randint(arg_keys[2], (TOKENS,), 0, LAYERS), jax.random.fold_in(arg_keys[2], 1), 0, LAYERS - 1).astype(jnp.int32)
    request_ids = touch_ends(jax.random.randint(arg_keys[3], (TOKENS,), 0, REQUESTS), jax.random.fold_in(arg_keys[3], 1), 0, REQUESTS - 1).astype(jnp.int32)
    target_resid = bell_draw(arg_keys[4], (TOKENS, D), 1.0, 6.0, ((0, 16),))
    decoder = bell_draw(arg_keys[5], (LAYERS, F, D), (KACT * PANEL) ** -0.5, 0.25, ((0, 2), (1, 16)))
    return dict(feature_codes=feature_codes, block_ids=block_ids, target_layer=target_layer, request_ids=request_ids, target_resid=target_resid, decoder=decoder)


def grouped(sorted_rows, weights, counts, starts, width):
    window_size = N_TOK * CAP
    total_rows = sorted_rows.shape[0]
    positions = jnp.arange(window_size, dtype=jnp.int32)

    def add_panel(buffer, panel_index):
        offset = starts[panel_index]
        window = lax.dynamic_slice_in_dim(sorted_rows, offset, window_size, 0)
        product = jnp.dot(window, weights[panel_index], preferred_element_type=jnp.float32)
        rounded = lax.optimization_barrier(product.astype(jnp.bfloat16)).astype(jnp.float32)
        keeping = positions < counts[panel_index]
        rounded = jnp.where(keeping[:, None], rounded, jnp.zeros_like(rounded))
        current = lax.dynamic_slice_in_dim(buffer, offset, window_size, 0)
        buffer = lax.dynamic_update_slice_in_dim(buffer, current + rounded, offset, 0)
        return (buffer, None)
    initial = jnp.zeros((total_rows, width), jnp.float32)
    buffer, _ = lax.scan(add_panel, initial, jnp.arange(PANELS, dtype=jnp.int32))
    return buffer[:total_rows - window_size]

def reference(feature_codes, block_ids, target_layer, request_ids, target_resid, decoder):
    count = target_resid.shape[0]
    row_total = count * KACT
    window_size = N_TOK * CAP
    panel_iota = jnp.arange(PANELS, dtype=jnp.int32)
    row_iota = jnp.arange(row_total, dtype=jnp.int32)
    rebuilt = jnp.zeros((count, D), jnp.float32)
    saved = []
    for source in range(LAYERS):
        alive_mask = (target_layer >= source).astype(feature_codes.dtype)
        masked = feature_codes[source] * alive_mask[:, None, None]
        flat_ids = block_ids[source].reshape(row_total).astype(jnp.int32)
        ranking = jnp.argsort(flat_ids, stable=True).astype(jnp.int32)
        inverse = jnp.zeros((row_total,), jnp.int32).at[ranking].set(row_iota)
        counts = lax.optimization_barrier(jnp.sum((flat_ids[:, None] == panel_iota[None, :]).astype(jnp.int32), axis=0)).astype(jnp.int32)
        starts = (jnp.cumsum(counts) - counts).astype(jnp.int32)
        code_rows = masked.reshape(row_total, PANEL)[ranking]
        code_rows = jnp.concatenate([code_rows, jnp.zeros((window_size, PANEL), code_rows.dtype)], axis=0)
        panels = decoder[source].reshape(PANELS, PANEL, D)
        contrib = grouped(code_rows, panels, counts, starts, D)[inverse]
        rebuilt = rebuilt + lax.optimization_barrier(jnp.sum(contrib.reshape(count, KACT, D), axis=1))
        saved.append((masked, ranking, inverse, counts, starts))
    error = target_resid.astype(jnp.float32) - rebuilt
    spread = lax.optimization_barrier(jnp.mean(error * error, axis=-1, keepdims=True))
    gradient = (error * lax.rsqrt(spread + 1e-06)).astype(jnp.bfloat16)
    members = (request_ids[:, None] == jnp.arange(REQUESTS, dtype=jnp.int32)[None, :]).astype(jnp.float32)
    scores = []
    totals = []
    for source in range(LAYERS):
        masked, ranking, inverse, counts, starts = saved[source]
        token_of = ranking // KACT
        grad_rows = jnp.concatenate([gradient[token_of], jnp.zeros((window_size, D), gradient.dtype)], axis=0)
        panels_t = jnp.swapaxes(decoder[source].reshape(PANELS, PANEL, D), 1, 2)
        projected = grouped(grad_rows, panels_t, counts, starts, PANEL)[inverse].reshape(count, KACT, PANEL)
        attribution = masked.astype(jnp.float32) * projected
        scores.append(attribution.astype(jnp.bfloat16))
        summed = jnp.zeros((REQUESTS * PANELS, PANEL), jnp.float32)
        for which in range(KACT):
            panel_hot = (block_ids[source][:, which][:, None] == panel_iota[None, :]).astype(jnp.float32)
            combined = (members[:, :, None] * panel_hot[:, None, :]).reshape(count, REQUESTS * PANELS)
            summed = summed + jnp.dot(combined.T, attribution[:, which], precision=lax.Precision.HIGHEST)
        totals.append(summed.reshape(REQUESTS, PANELS * PANEL))
    return (jnp.stack(scores, axis=0), jnp.stack(totals, axis=1))
```

```python
import jax
import jax.numpy as jnp
from jax import lax
from jax.sharding import PartitionSpec as P

REQUESTS = 16


def per_device(feature_codes, block_ids, target_layer, request_ids, target_resid, decoder):
    layers_here, count, kact, panel = feature_codes.shape
    width = target_resid.shape[1]
    features = decoder.shape[1]
    per_dev = features // panel
    tok, lyr = lax.axis_index("tok"), lax.axis_index("lyr")
    lyr_count = lax.axis_size("lyr")
    layer_ids = lyr * layers_here + jnp.arange(layers_here, dtype=jnp.int32)
    alive = layer_ids[:, None] <= target_layer[None, :]
    masked = jnp.where(alive[:, :, None, None], feature_codes, jnp.zeros_like(feature_codes))
    all_codes = lax.all_gather(masked, "tok", axis=1, tiled=True)
    all_ids = lax.all_gather(block_ids, "tok", axis=1, tiled=True)
    all_requests = lax.all_gather(request_ids, "tok", axis=0, tiled=True)
    mine = tok * per_dev + jnp.arange(per_dev, dtype=jnp.int32)
    named = (all_ids[..., None] == mine).astype(jnp.bfloat16)
    dense = jnp.sum(all_codes[:, :, :, None, :] * named[..., None], axis=2)
    tokens = dense.shape[1]
    dense = jnp.swapaxes(dense, 0, 1).reshape(tokens, layers_here * features)
    weights = decoder.reshape(layers_here * features, width)
    partial = jnp.dot(dense, weights, preferred_element_type=jnp.float32).astype(jnp.bfloat16)
    rebuilt = lax.psum_scatter(partial, ("tok", "lyr"), scatter_dimension=0, tiled=True)
    rows = count // lyr_count
    resid = lax.dynamic_slice_in_dim(target_resid, lyr * rows, rows, 0)
    error = resid.astype(jnp.float32) - rebuilt.astype(jnp.float32)
    spread = jnp.mean(error * error, axis=-1, keepdims=True)
    gradient = (error * lax.rsqrt(spread + 1e-06)).astype(jnp.bfloat16)
    gradients = lax.all_gather(gradient, ("tok", "lyr"), axis=0, tiled=True)
    projected = lax.dot_general(
        gradients, weights, (((1,), (1,)), ((), ())), preferred_element_type=jnp.float32
    ).astype(jnp.bfloat16)
    attribution = dense.astype(jnp.float32) * projected.astype(jnp.float32)
    members = (all_requests[:, None] == jnp.arange(REQUESTS, dtype=jnp.int32)).astype(jnp.float32)
    totals = lax.dot_general(
        members, attribution, (((0,), (0,)), ((), ())), precision=lax.Precision.HIGHEST
    ).reshape(REQUESTS, layers_here, features)
    scored = attribution.astype(jnp.bfloat16).reshape(tokens, layers_here, 1, per_dev, panel)
    spread_out = jnp.sum(
        scored * jnp.swapaxes(named, 0, 1)[..., None], axis=3
    )
    scores = lax.psum_scatter(
        jnp.swapaxes(spread_out, 0, 1), "tok", scatter_dimension=1, tiled=True
    )
    return (scores, totals)


def solution(mesh):
    placed = (
        P("lyr", "tok", None, None),
        P("lyr", "tok", None),
        P("tok"),
        P("tok"),
        P("tok", None),
        P("lyr", "tok", None),
    )
    return jax.shard_map(
        per_device,
        mesh=mesh,
        in_specs=placed,
        out_specs=(P("lyr", "tok", None, None), P(None, "lyr", "tok")),
        check_vma=False,
    )
```

```python
import functools

import jax
import jax.numpy as jnp
from jax import lax
from jax.experimental import pallas as pl
from jax.experimental.pallas import tpu as pltpu
from jax.sharding import PartitionSpec as P

REQUESTS = 16
MESH = pl.DeviceIdType.MESH


class Place:
    def __init__(self):
        tok, y = lax.axis_index("tok"), lax.axis_index("lyr")
        z, x, c = tok // 4, (tok // 2) % 2, tok % 2
        self.z, self.c = z, c
        self.inner = (z % 3) != 0
        self.first = (1 - c) * y + c * x
        self.second = (1 - c) * x + c * y
        across_x, across_y = (tok + 2 - 4 * x, y), (tok, 1 - y)
        self.to_first = tuple((1 - c) * a + c * b for a, b in zip(across_y, across_x))
        self.to_second = tuple((1 - c) * a + c * b for a, b in zip(across_x, across_y))
        self.to_core = (tok + 1 - 2 * c, y)
        self.tok, self.y = tok, y
        half = z // 2
        self.near = [z, z + 1 - 2 * (z % 2), 2 - half, 3 - 3 * half]

    def along(self, step):
        return (self.tok + 4 * step, self.y)

    def quarter(self, first, second):
        return (1 - self.c) * (second * 2 + first) + self.c * (first * 2 + second)

    def barrier(self):
        gate = pltpu.get_barrier_semaphore()
        for target in (self.to_first, self.to_second, self.to_core):
            pl.semaphore_signal(gate, inc=1, device_id=target, device_id_type=MESH)

        @pl.when(self.z > 0)
        def _():
            pl.semaphore_signal(gate, inc=1, device_id=self.along(-1), device_id_type=MESH)

        @pl.when(self.z < 3)
        def _():
            pl.semaphore_signal(gate, inc=1, device_id=self.along(1), device_id_type=MESH)

        pl.semaphore_wait(gate, 4 + (self.z % 3 + 1) // 2)


def remote(src, dst, send, recv, target):
    return pltpu.make_async_remote_copy(
        src_ref=src, dst_ref=dst, send_sem=send, recv_sem=recv, device_id=target, device_id_type=MESH
    )


def gather_kernel(own_ref, out_ref, local_sem, recv_sem, core_sem, first_sem, second_sem, z_sem):
    at = Place()
    at.barrier()

    def block(z, first, second, core):
        return (z * 2 + core) * 4 + at.quarter(first, second)

    def mine(j, flip_first, flip_second):
        f = 1 - at.first if flip_first else at.first
        s = 1 - at.second if flip_second else at.second
        return block(at.near[j], f, s, at.c)

    def send(b, sem, target):
        remote(out_ref.at[b], out_ref.at[b], sem, recv_sem.at[b], target).start()

    def arrived(b):
        remote(out_ref.at[b], out_ref.at[b], core_sem.at[0], recv_sem.at[b], at.to_core).wait_recv()

    b0 = mine(0, False, False)
    keep = pltpu.make_async_copy(own_ref, out_ref.at[b0], local_sem)
    keep.start()
    keep.wait()
    used = [0, 0, 0]

    def fan(b, second, first):
        if second:
            send(b, second_sem.at[used[1]], at.to_second)
            used[1] += 1
        if first:
            send(b, first_sem.at[used[0]], at.to_first)
            used[0] += 1
        send(b, core_sem.at[used[2]], at.to_core)
        used[2] += 1

    @pl.when(at.z > 0)
    def _():
        send(b0, z_sem.at[0], at.along(-1))

    @pl.when(at.z < 3)
    def _():
        send(b0, z_sem.at[1], at.along(1))

    fan(b0, True, True)

    def from_z(j):
        b = mine(j, False, False)
        arrived(b)
        step = (3 - 2 * at.z) if j == 1 else (2 * at.z - 3)

        @pl.when(at.inner)
        def _():
            send(b, z_sem.at[1 + j], at.along(step))

        fan(b, True, True)

    def from_second(j):
        b = mine(j, False, True)
        arrived(b)
        fan(b, False, True)

    def from_first(j, flip):
        b = mine(j, True, flip)
        arrived(b)
        fan(b, False, False)

    from_second(0)
    from_z(1)
    from_first(0, False)
    from_second(1)
    from_z(2)
    from_first(0, True)
    from_first(1, False)
    from_second(2)
    from_z(3)
    from_first(1, True)
    from_first(2, False)
    from_second(3)
    from_first(2, True)
    from_first(3, False)
    from_first(3, True)
    for z in range(4):
        for q in range(4):
            arrived((z * 2 + 1 - at.c) * 4 + q)
    for i in range(16):
        remote(own_ref, own_ref, core_sem.at[i], recv_sem.at[0], at.to_core).wait_send()
    for i in range(8):
        remote(own_ref, own_ref, first_sem.at[i], recv_sem.at[0], at.to_core).wait_send()
    for i in range(4):
        remote(own_ref, own_ref, second_sem.at[i], recv_sem.at[0], at.to_core).wait_send()

    @pl.when(at.z > 0)
    def _():
        remote(own_ref, own_ref, z_sem.at[0], recv_sem.at[0], at.to_core).wait_send()

    @pl.when(at.z < 3)
    def _():
        remote(own_ref, own_ref, z_sem.at[1], recv_sem.at[0], at.to_core).wait_send()

    @pl.when(at.inner)
    def _():
        for i in range(2, 5):
            remote(own_ref, own_ref, z_sem.at[i], recv_sem.at[0], at.to_core).wait_send()


def gather_rows(own):
    rows, width = own.shape
    dma = pltpu.SemaphoreType.DMA
    out = pl.pallas_call(
        gather_kernel,
        out_shape=jax.ShapeDtypeStruct((32, rows, width), own.dtype),
        in_specs=[pl.BlockSpec(memory_space=pltpu.VMEM)],
        out_specs=pl.BlockSpec(memory_space=pltpu.VMEM),
        scratch_shapes=[dma, dma((32,)), dma((16,)), dma((8,)), dma((4,)), dma((5,))],
        compiler_params=pltpu.CompilerParams(collective_id=1, has_side_effects=True),
        name="gather_rows",
    )(own)
    return out


def reduce_kernel(
    codes_ref, weights_ref, resid_ref, out_ref,
    held, core_out, core_in, first_out, first_in, second_out, second_in, z_out, z_in,
    core_send, core_recv, first_send, first_recv, second_send, second_recv, z_send, z_recv,
):
    at = Place()
    at.barrier()
    rows, width = out_ref.shape
    depth = codes_ref.shape[-1]
    tile = 256 if width % 256 == 0 else width
    far = at.near[::-1]

    def product(i):
        for core in (1 - at.c, at.c):
            left = codes_ref[far[i] * 2 + core].reshape(4 * rows, depth)
            away = core is not at.c

            @pl.loop(0, width // tile)
            def _(n):
                cols = pl.ds(pl.multiple_of(n * tile, tile), tile)
                value = jnp.dot(left, weights_ref[:, cols], preferred_element_type=jnp.float32)
                value = value.reshape(4, rows, tile)
                if away:
                    core_out[i, :, :, cols] = value.astype(core_out.dtype)
                else:
                    held[i, :, :, cols] = value

            if away:
                core_copy(i).start()

    def core_copy(i):
        return remote(core_out.at[i], core_in.at[i], core_send.at[i], core_recv.at[i], at.to_core)

    def first_copy(i, k):
        return remote(first_out.at[i, k], first_in.at[i, k], first_send.at[i, k], first_recv.at[i, k], at.to_first)

    def second_copy(i):
        return remote(second_out.at[i], second_in.at[i], second_send.at[i], second_recv.at[i], at.to_second)

    def z_copy(i, way, step):
        slot = way * 4 + far[i]
        return remote(z_out.at[i], z_in.at[slot], z_send.at[i], z_recv.at[slot], at.along(step))

    def f32(v):
        return v.astype(jnp.float32)

    def both(i, q):
        return held[i, q] + f32(core_in[i, q])

    def spot(k):
        return 1 - at.second if k == 0 else at.second

    def over_first(i):
        core_copy(i).wait_recv()
        for k in (0, 1):
            first_out[i, k] = both(i, at.quarter(1 - at.first, spot(k))).astype(first_out.dtype)
            first_copy(i, k).start()

    def over_second(i):
        first_copy(i, 0).wait_recv()
        total = both(i, at.quarter(at.first, spot(0))) + f32(first_in[i, 0])
        second_out[i] = total.astype(second_out.dtype)
        second_copy(i).start()

    def z_arrived(slot):
        remote(z_in.at[slot], z_in.at[slot], z_send.at[0], z_recv.at[slot], at.to_core).wait_recv()

    def along_z(i):
        first_copy(i, 1).wait_recv()
        second_copy(i).wait_recv()
        q = at.quarter(at.first, at.second)
        total = both(i, q) + f32(first_in[i, 1]) + f32(second_in[i])
        held[i, q] = total
        if i < 3:
            way = (at.z // 2) if i < 2 else (at.z % 2)
            slot = way * 4 + far[i]

            @pl.when(at.inner)
            def _():
                z_arrived(slot)
                z_out[i] = (held[i, q] + f32(z_in[slot])).astype(z_out.dtype)

            @pl.when(jnp.logical_not(at.inner))
            def _():
                z_out[i] = held[i, q].astype(z_out.dtype)

            z_copy(i, way, 1 - 2 * way).start()
        else:
            @pl.when(at.z > 0)
            def _():
                z_arrived(at.z)
                held[i, q] += f32(z_in[at.z])

            @pl.when(at.z < 3)
            def _():
                z_arrived(4 + at.z)
                held[i, q] += f32(z_in[4 + at.z])

            error = f32(resid_ref[...]) - held[i, q]
            spread = jnp.mean(error * error, axis=-1, keepdims=True)
            out_ref[...] = (error * lax.rsqrt(spread + 1e-06)).astype(out_ref.dtype)

    product(0)
    product(1)
    over_first(0)
    product(2)
    over_first(1)
    over_second(0)
    product(3)
    over_first(2)
    over_second(1)
    along_z(0)
    over_first(3)
    over_second(2)
    along_z(1)
    over_second(3)
    along_z(2)
    along_z(3)
    for i in range(4):
        core_copy(i).wait_send()
        first_copy(i, 0).wait_send()
        first_copy(i, 1).wait_send()
        second_copy(i).wait_send()
        if i < 3:
            remote(z_out.at[i], z_out.at[i], z_send.at[i], z_recv.at[0], at.to_core).wait_send()


def reduce_rows(codes, weights, resid):
    rows, width = resid.shape
    depth = codes.shape[-1]
    dma, bf16 = pltpu.SemaphoreType.DMA, jnp.bfloat16
    vmem = pl.BlockSpec(memory_space=pltpu.VMEM)
    block = (rows, width)
    return pl.pallas_call(
        reduce_kernel,
        out_shape=jax.ShapeDtypeStruct(block, bf16),
        in_specs=[vmem] * 3,
        out_specs=vmem,
        scratch_shapes=[
            pltpu.VMEM((4, 4) + block, jnp.float32),
            pltpu.VMEM((4, 4) + block, bf16),
            pltpu.VMEM((4, 4) + block, bf16),
            pltpu.VMEM((4, 2) + block, bf16),
            pltpu.VMEM((4, 2) + block, bf16),
            pltpu.VMEM((4,) + block, bf16),
            pltpu.VMEM((4,) + block, bf16),
            pltpu.VMEM((3,) + block, bf16),
            pltpu.VMEM((8,) + block, bf16),
            dma((4,)), dma((4,)), dma((4, 2)), dma((4, 2)), dma((4,)), dma((4,)), dma((3,)), dma((8,)),
        ],
        compiler_params=pltpu.CompilerParams(
            collective_id=2, has_side_effects=True, vmem_limit_bytes=60 * 1024 * 1024
        ),
        name="reduce_rows",
    )(codes, weights, resid)


def blocked(table, rows):
    rest = table.shape[1:]
    return jnp.swapaxes(table.reshape((4, 2, 2, 2, rows) + rest), 1, 2).reshape((8, 4, rows) + rest)


def unblocked(table):
    rows, rest = table.shape[1], table.shape[2:]
    return jnp.swapaxes(table.reshape((4, 2, 2, 2, rows) + rest), 1, 2).reshape((32 * rows,) + rest)


def per_device(feature_codes, block_ids, target_layer, request_ids, target_resid, decoder, grid=False):
    layers_here, count, kact, panel = feature_codes.shape
    width = target_resid.shape[1]
    features = decoder.shape[1]
    per_dev = features // panel
    tok, lyr = lax.axis_index("tok"), lax.axis_index("lyr")
    lyr_count = lax.axis_size("lyr")
    layer_ids = lyr * layers_here + jnp.arange(layers_here, dtype=jnp.int32)
    alive = layer_ids[:, None] <= target_layer[None, :]
    masked = jnp.where(alive[:, :, None, None], feature_codes, jnp.zeros_like(feature_codes))
    all_codes = lax.all_gather(masked, "tok", axis=1, tiled=True)
    numbers = jnp.concatenate(
        [jnp.moveaxis(block_ids, 1, 2).reshape(layers_here * kact, count), request_ids[None, :]], axis=0
    )
    numbers = lax.all_gather(numbers, "tok", axis=1, tiled=True)
    all_ids = jnp.moveaxis(numbers[:-1].reshape(layers_here, kact, -1), 1, 2)
    all_requests = numbers[-1]
    mine = tok * per_dev + jnp.arange(per_dev, dtype=jnp.int32)
    named = (all_ids[..., None] == mine).astype(jnp.bfloat16)
    dense = jnp.sum(all_codes[:, :, :, None, :] * named[..., None], axis=2)
    tokens = dense.shape[1]
    dense = jnp.swapaxes(dense, 0, 1).reshape(tokens, layers_here * features)
    weights = decoder.reshape(layers_here * features, width)
    rows = count // lyr_count
    resid = lax.dynamic_slice_in_dim(target_resid, lyr * rows, rows, 0)
    if grid:
        gradient = reduce_rows(blocked(dense, rows), weights, resid)
        gradients = unblocked(gather_rows(gradient))
    else:
        partial = jnp.dot(dense, weights, preferred_element_type=jnp.float32).astype(jnp.bfloat16)
        rebuilt = lax.psum_scatter(partial, ("tok", "lyr"), scatter_dimension=0, tiled=True)
        error = resid.astype(jnp.float32) - rebuilt.astype(jnp.float32)
        spread = jnp.mean(error * error, axis=-1, keepdims=True)
        gradient = (error * lax.rsqrt(spread + 1e-06)).astype(jnp.bfloat16)
        gradients = lax.all_gather(gradient, ("tok", "lyr"), axis=0, tiled=True)
    projected = lax.dot_general(
        gradients, weights, (((1,), (1,)), ((), ())), preferred_element_type=jnp.float32
    ).astype(jnp.bfloat16)
    attribution = dense.astype(jnp.float32) * projected.astype(jnp.float32)
    members = (all_requests[:, None] == jnp.arange(REQUESTS, dtype=jnp.int32)).astype(jnp.float32)
    totals = lax.dot_general(
        members, attribution, (((0,), (0,)), ((), ())), precision=lax.Precision.HIGHEST
    ).reshape(REQUESTS, layers_here, features)
    scored = attribution.astype(jnp.bfloat16).reshape(tokens, layers_here, 1, per_dev, panel)
    spread_out = jnp.sum(
        scored * jnp.swapaxes(named, 0, 1)[..., None], axis=3
    )
    scores = lax.psum_scatter(
        jnp.swapaxes(spread_out, 0, 1), "tok", scatter_dimension=1, tiled=True
    )
    return (scores, totals)


def solution(mesh):
    placed = (
        P("lyr", "tok", None, None),
        P("lyr", "tok", None),
        P("tok"),
        P("tok"),
        P("tok", None),
        P("lyr", "tok", None),
    )
    wide = len({getattr(d, "coords", (0,))[0] for d in mesh.devices.flat})
    grid = (mesh.shape["tok"], mesh.shape["lyr"]) == (16, 2) and wide == 2
    return jax.shard_map(
        functools.partial(per_device, grid=grid),
        mesh=mesh,
        in_specs=placed,
        out_specs=(P("lyr", "tok", None, None), P(None, "lyr", "tok")),
        check_vma=False,
    )
```

```python
import functools

import jax
import jax.numpy as jnp
from jax import lax
from jax.experimental import pallas as pl
from jax.experimental.pallas import tpu as pltpu
from jax.sharding import PartitionSpec as P

REQUESTS = 16
CAP = 16
MESH = pl.DeviceIdType.MESH


class Place:
    def __init__(self):
        tok, y = lax.axis_index("tok"), lax.axis_index("lyr")
        z, x, c = tok // 4, (tok // 2) % 2, tok % 2
        self.z, self.c = z, c
        self.inner = (z % 3) != 0
        self.first = (1 - c) * y + c * x
        self.second = (1 - c) * x + c * y
        across_x, across_y = (tok + 2 - 4 * x, y), (tok, 1 - y)
        self.to_first = tuple((1 - c) * a + c * b for a, b in zip(across_y, across_x))
        self.to_second = tuple((1 - c) * a + c * b for a, b in zip(across_x, across_y))
        self.to_core = (tok + 1 - 2 * c, y)
        self.tok, self.y = tok, y
        half = z // 2
        self.near = [z, z + 1 - 2 * (z % 2), 2 - half, 3 - 3 * half]

    def along(self, step):
        return (self.tok + 4 * step, self.y)

    def quarter(self, first, second):
        return (1 - self.c) * (second * 2 + first) + self.c * (first * 2 + second)

    def peer(self, distance):
        return ((self.tok + distance) % 16, self.y)

    def barrier(self):
        gate = pltpu.get_barrier_semaphore()
        for distance in range(1, 16):
            pl.semaphore_signal(gate, inc=1, device_id=self.peer(distance), device_id_type=MESH)
        pl.semaphore_signal(gate, inc=1, device_id=(self.tok, 1 - self.y), device_id_type=MESH)
        pl.semaphore_wait(gate, 16)


def earlier(count):
    shape = (count, count)
    return (lax.broadcasted_iota(jnp.int32, shape, 0) < lax.broadcasted_iota(jnp.int32, shape, 1)).astype(jnp.bfloat16)


def slots(numbers, layer, first_panel, panels):
    shape = (panels * CAP, numbers.shape[1])
    row = lax.broadcasted_iota(jnp.int32, shape, 0)
    panel = row // CAP + first_panel
    rank = (row % CAP).astype(jnp.float32)
    named = [numbers[2 * layer + k : 2 * layer + k + 1] == panel for k in (0, 1)]
    either = jnp.where(named[0] | named[1], 1.0, 0.0).astype(jnp.bfloat16)
    before = jnp.dot(either, earlier(shape[1]), preferred_element_type=jnp.float32)
    here = before == rank
    return [jnp.where(n & here, 1.0, 0.0).astype(jnp.bfloat16) for n in named]


def remote(src, dst, send, recv, target):
    return pltpu.make_async_remote_copy(
        src_ref=src, dst_ref=dst, send_sem=send, recv_sem=recv, device_id=target, device_id_type=MESH
    )


def gather_kernel(
    own_ref, dense_ref, weights_ref, numbers_ref, local_numbers_ref, scores_ref, totals_ref,
    out_ref, slot_out, slot_in, local_sem, recv_sem, core_sem, first_sem, second_sem, z_sem, slot_send, slot_recv,
):
    at = Place()
    at.barrier()

    def block(z, first, second, core):
        return (z * 2 + core) * 4 + at.quarter(first, second)

    def mine(j, flip_first, flip_second):
        f = 1 - at.first if flip_first else at.first
        s = 1 - at.second if flip_second else at.second
        return block(at.near[j], f, s, at.c)

    def send(b, sem, target):
        remote(out_ref.at[b], out_ref.at[b], sem, recv_sem.at[b], target).start()

    def arrived(b):
        remote(out_ref.at[b], out_ref.at[b], core_sem.at[0], recv_sem.at[b], at.to_core).wait_recv()

    b0 = mine(0, False, False)
    keep = pltpu.make_async_copy(own_ref, out_ref.at[b0], local_sem)
    keep.start()
    keep.wait()
    used = [0, 0, 0]

    def fan(b, second, first):
        if second:
            send(b, second_sem.at[used[1]], at.to_second)
            used[1] += 1
        if first:
            send(b, first_sem.at[used[0]], at.to_first)
            used[0] += 1
        send(b, core_sem.at[used[2]], at.to_core)
        used[2] += 1

    @pl.when(at.z > 0)
    def _():
        send(b0, z_sem.at[0], at.along(-1))

    @pl.when(at.z < 3)
    def _():
        send(b0, z_sem.at[1], at.along(1))

    fan(b0, True, True)

    def from_z(j):
        b = mine(j, False, False)
        arrived(b)
        step = (3 - 2 * at.z) if j == 1 else (2 * at.z - 3)

        @pl.when(at.inner)
        def _():
            send(b, z_sem.at[1 + j], at.along(step))

        fan(b, True, True)

    def from_second(j):
        b = mine(j, False, True)
        arrived(b)
        fan(b, False, True)

    def from_first(j, flip):
        b = mine(j, True, flip)
        arrived(b)
        fan(b, False, False)

    rows = out_ref.shape[1]
    panel = slot_out.shape[-1]
    totals_ref[...] = jnp.zeros_like(totals_ref)

    def slot_copy(source):
        return remote(
            slot_out.at[source], slot_in.at[at.tok], slot_send.at[source], slot_recv.at[at.tok], (source, at.y)
        )

    def project(z, core, own):
        group = z * 2 + core
        left = out_ref[pl.ds(group * 4, 4)].reshape(4 * rows, out_ref.shape[2])
        sources = [(z * 2 + x) * 2 + core for x in (0, 1)]
        numbers = [numbers_ref[source] for source in sources]
        members = []
        for x in (0, 1):
            wanted = lax.broadcasted_iota(jnp.int32, (REQUESTS, 2 * rows), 0)
            members.append(jnp.where(numbers[x][4:5] == wanted, 1.0, 0.0).astype(jnp.bfloat16))
        for n in range(4):
            layer, which = n // 2, n % 2
            cols = slice(n * panel, (n + 1) * panel)
            product = lax.dot_general(
                left, weights_ref[cols, :], (((1,), (1,)), ((), ())), preferred_element_type=jnp.float32
            ).astype(jnp.bfloat16)
            for x in (0, 1):
                span = slice(x * 2 * rows, (x + 1) * 2 * rows)
                value = product[span].astype(jnp.float32) * dense_ref[group, x, :, cols].astype(jnp.float32)
                high = value.astype(jnp.bfloat16)
                low = (value - high.astype(jnp.float32)).astype(jnp.bfloat16)
                totals_ref[:, cols] += jnp.dot(members[x], high, preferred_element_type=jnp.float32) + jnp.dot(
                    members[x], low, preferred_element_type=jnp.float32
                )
                held = slots(numbers[x], layer, at.tok * 2 + which, 1)
                packed = jnp.dot(held[0] + held[1], high, preferred_element_type=jnp.float32).astype(jnp.bfloat16)
                slot_out[sources[x], layer, which * CAP : (which + 1) * CAP, :] = packed
        for x in (0, 1):
            if own:

                @pl.when(sources[x] != at.tok)
                def _():
                    slot_copy(sources[x]).start()

            else:
                slot_copy(sources[x]).start()

    def from_core(j):
        for q in range(4):
            arrived((at.near[j] * 2 + 1 - at.c) * 4 + q)
        project(at.near[j], 1 - at.c, False)

    from_second(0)
    from_z(1)
    from_first(0, False)
    from_second(1)
    from_z(2)
    from_first(0, True)
    from_first(1, False)
    from_second(2)
    from_z(3)
    from_first(1, True)
    project(at.near[0], at.c, True)
    from_first(2, False)
    from_second(3)
    from_core(0)
    project(at.near[1], at.c, False)
    from_first(2, True)
    project(at.near[2], at.c, False)
    from_first(3, False)
    from_core(1)
    from_first(3, True)
    from_core(2)
    project(at.near[3], at.c, False)
    from_core(3)
    slot_in[at.tok] = slot_out[at.tok]
    for distance in range(1, 16):
        source = (at.tok + distance) % 16
        remote(
            slot_out.at[0], slot_in.at[source], slot_send.at[0], slot_recv.at[source], at.to_core
        ).wait_recv()
    for layer in (0, 1):
        held = slots(local_numbers_ref[...], layer, 0, 32)
        table = slot_in[:, layer].reshape(32 * CAP, panel)
        for k in (0, 1):
            scores_ref[2 * layer + k] = lax.dot_general(
                held[k], table, (((0,), (0,)), ((), ())), preferred_element_type=jnp.float32
            ).astype(scores_ref.dtype)
    for distance in range(1, 16):
        source = (at.tok + distance) % 16
        remote(
            slot_out.at[0], slot_in.at[0], slot_send.at[source], slot_recv.at[0], at.to_core
        ).wait_send()
    for i in range(16):
        remote(own_ref, own_ref, core_sem.at[i], recv_sem.at[0], at.to_core).wait_send()
    for i in range(8):
        remote(own_ref, own_ref, first_sem.at[i], recv_sem.at[0], at.to_core).wait_send()
    for i in range(4):
        remote(own_ref, own_ref, second_sem.at[i], recv_sem.at[0], at.to_core).wait_send()

    @pl.when(at.z > 0)
    def _():
        remote(own_ref, own_ref, z_sem.at[0], recv_sem.at[0], at.to_core).wait_send()

    @pl.when(at.z < 3)
    def _():
        remote(own_ref, own_ref, z_sem.at[1], recv_sem.at[0], at.to_core).wait_send()

    @pl.when(at.inner)
    def _():
        for i in range(2, 5):
            remote(own_ref, own_ref, z_sem.at[i], recv_sem.at[0], at.to_core).wait_send()


def gather_rows(own, dense, weights, numbers, local_numbers, panel):
    rows, width = own.shape
    dma, bf16 = pltpu.SemaphoreType.DMA, jnp.bfloat16
    vmem = pl.BlockSpec(memory_space=pltpu.VMEM)
    return pl.pallas_call(
        gather_kernel,
        out_shape=(
            jax.ShapeDtypeStruct((4, 2 * rows, panel), bf16),
            jax.ShapeDtypeStruct((REQUESTS, weights.shape[0]), jnp.float32),
        ),
        in_specs=[vmem] * 5,
        out_specs=(vmem, vmem),
        scratch_shapes=[
            pltpu.VMEM((32, rows, width), bf16),
            pltpu.VMEM((16, 2, 2 * CAP, panel), bf16),
            pltpu.VMEM((16, 2, 2 * CAP, panel), bf16),
            dma, dma((32,)), dma((16,)), dma((8,)), dma((4,)), dma((5,)), dma((16,)), dma((16,)),
        ],
        compiler_params=pltpu.CompilerParams(
            collective_id=1, has_side_effects=True, vmem_limit_bytes=60 * 1024 * 1024
        ),
        name="gather_rows",
    )(own, dense, weights, numbers, local_numbers)


def reduce_kernel(
    masked_ref, local_numbers_ref, weights_ref, resid_ref, out_ref, codes_ref, numbers_ref,
    packed, slot_in, slot_send, slot_recv, number_send, number_recv, held, core_out, core_in, first_out, first_in, second_out, second_in, z_out, z_in,
    core_send, core_recv, first_send, first_recv, second_send, second_recv, z_send, z_recv,
):
    at = Place()
    at.barrier()
    rows, width = out_ref.shape
    depth = codes_ref.shape[-1]
    panel = packed.shape[-1]
    local = local_numbers_ref[...]
    numbers_ref[at.tok] = local
    for layer in (0, 1):
        sent = slots(local, layer, 0, 32)
        value = sum(
            jnp.dot(sent[k], masked_ref[2 * layer + k], preferred_element_type=jnp.float32) for k in (0, 1)
        )
        packed[:, layer] = value.astype(packed.dtype).reshape(16, 2 * CAP, panel)

    def slot_copies(distance):
        target = (at.tok + distance) % 16
        return (
            remote(
                packed.at[target], slot_in.at[at.tok], slot_send.at[distance], slot_recv.at[distance], (target, at.y)
            ),
            remote(
                local_numbers_ref, numbers_ref.at[at.tok], number_send.at[distance], number_recv.at[distance],
                (target, at.y),
            ),
        )

    for distance in range(1, 16):
        for copy in slot_copies(distance):
            copy.start()
    slot_in[at.tok] = packed[at.tok]
    for distance in range(1, 16):
        for copy in slot_copies(distance):
            copy.wait_recv()

    @pl.loop(0, 16)
    def _(source):
        for layer in (0, 1):
            held_slots = slots(numbers_ref[source], layer, at.tok * 2, 2)
            hot = held_slots[0] + held_slots[1]
            for which in (0, 1):
                part = slice(which * CAP, (which + 1) * CAP)
                n = 2 * layer + which
                codes_ref[(source // 4) * 2 + source % 2, (source // 2) % 2, :, n * panel : (n + 1) * panel] = (
                    lax.dot_general(
                        hot[part], slot_in[source, layer, part, :], (((0,), (0,)), ((), ())),
                        preferred_element_type=jnp.float32,
                    ).astype(codes_ref.dtype)
                )

    tile = 256 if width % 256 == 0 else width
    far = at.near[::-1]

    def product(i):
        for core in (1 - at.c, at.c):
            left = codes_ref[far[i] * 2 + core].reshape(4 * rows, depth)
            away = core is not at.c

            @pl.loop(0, width // tile)
            def _(n):
                cols = pl.ds(pl.multiple_of(n * tile, tile), tile)
                value = jnp.dot(left, weights_ref[:, cols], preferred_element_type=jnp.float32)
                value = value.reshape(4, rows, tile)
                if away:
                    core_out[i, :, :, cols] = value.astype(core_out.dtype)
                else:
                    held[i, :, :, cols] = value

            if away:
                core_copy(i).start()

    def core_copy(i):
        return remote(core_out.at[i], core_in.at[i], core_send.at[i], core_recv.at[i], at.to_core)

    def first_copy(i, k):
        return remote(first_out.at[i, k], first_in.at[i, k], first_send.at[i, k], first_recv.at[i, k], at.to_first)

    def second_copy(i):
        return remote(second_out.at[i], second_in.at[i], second_send.at[i], second_recv.at[i], at.to_second)

    def z_copy(i, way, step):
        slot = way * 4 + far[i]
        return remote(z_out.at[i], z_in.at[slot], z_send.at[i], z_recv.at[slot], at.along(step))

    def f32(v):
        return v.astype(jnp.float32)

    def both(i, q):
        return held[i, q] + f32(core_in[i, q])

    def spot(k):
        return 1 - at.second if k == 0 else at.second

    def over_first(i):
        core_copy(i).wait_recv()
        for k in (0, 1):
            first_out[i, k] = both(i, at.quarter(1 - at.first, spot(k))).astype(first_out.dtype)
            first_copy(i, k).start()

    def over_second(i):
        first_copy(i, 0).wait_recv()
        total = both(i, at.quarter(at.first, spot(0))) + f32(first_in[i, 0])
        second_out[i] = total.astype(second_out.dtype)
        second_copy(i).start()

    def z_arrived(slot):
        remote(z_in.at[slot], z_in.at[slot], z_send.at[0], z_recv.at[slot], at.to_core).wait_recv()

    def along_z(i):
        first_copy(i, 1).wait_recv()
        second_copy(i).wait_recv()
        q = at.quarter(at.first, at.second)
        total = both(i, q) + f32(first_in[i, 1]) + f32(second_in[i])
        held[i, q] = total
        if i < 3:
            way = (at.z // 2) if i < 2 else (at.z % 2)
            slot = way * 4 + far[i]

            @pl.when(at.inner)
            def _():
                z_arrived(slot)
                z_out[i] = (held[i, q] + f32(z_in[slot])).astype(z_out.dtype)

            @pl.when(jnp.logical_not(at.inner))
            def _():
                z_out[i] = held[i, q].astype(z_out.dtype)

            z_copy(i, way, 1 - 2 * way).start()
        else:
            @pl.when(at.z > 0)
            def _():
                z_arrived(at.z)
                held[i, q] += f32(z_in[at.z])

            @pl.when(at.z < 3)
            def _():
                z_arrived(4 + at.z)
                held[i, q] += f32(z_in[4 + at.z])

            error = f32(resid_ref[...]) - held[i, q]
            spread = jnp.mean(error * error, axis=-1, keepdims=True)
            out_ref[...] = (error * lax.rsqrt(spread + 1e-06)).astype(out_ref.dtype)

    product(0)
    product(1)
    over_first(0)
    product(2)
    over_first(1)
    over_second(0)
    product(3)
    over_first(2)
    over_second(1)
    along_z(0)
    over_first(3)
    over_second(2)
    along_z(1)
    over_second(3)
    along_z(2)
    along_z(3)
    for distance in range(1, 16):
        for copy in slot_copies(distance):
            copy.wait_send()
    for i in range(4):
        core_copy(i).wait_send()
        first_copy(i, 0).wait_send()
        first_copy(i, 1).wait_send()
        second_copy(i).wait_send()
        if i < 3:
            remote(z_out.at[i], z_out.at[i], z_send.at[i], z_recv.at[0], at.to_core).wait_send()


def reduce_rows(masked, local_numbers, weights, resid):
    rows, width = resid.shape
    depth = weights.shape[0]
    panel = masked.shape[-1]
    dma, bf16 = pltpu.SemaphoreType.DMA, jnp.bfloat16
    vmem = pl.BlockSpec(memory_space=pltpu.VMEM)
    block = (rows, width)
    return pl.pallas_call(
        reduce_kernel,
        out_shape=(
            jax.ShapeDtypeStruct(block, bf16),
            jax.ShapeDtypeStruct((8, 2, 2 * rows, depth), bf16),
            jax.ShapeDtypeStruct((16,) + local_numbers.shape, jnp.int32),
        ),
        in_specs=[vmem] * 4,
        out_specs=(vmem,) * 3,
        scratch_shapes=[
            pltpu.VMEM((16, 2, 2 * CAP, panel), bf16),
            pltpu.VMEM((16, 2, 2 * CAP, panel), bf16),
            dma((16,)), dma((16,)), dma((16,)), dma((16,)),
            pltpu.VMEM((4, 4) + block, jnp.float32),
            pltpu.VMEM((4, 4) + block, bf16),
            pltpu.VMEM((4, 4) + block, bf16),
            pltpu.VMEM((4, 2) + block, bf16),
            pltpu.VMEM((4, 2) + block, bf16),
            pltpu.VMEM((4,) + block, bf16),
            pltpu.VMEM((4,) + block, bf16),
            pltpu.VMEM((3,) + block, bf16),
            pltpu.VMEM((8,) + block, bf16),
            dma((4,)), dma((4,)), dma((4, 2)), dma((4, 2)), dma((4,)), dma((4,)), dma((3,)), dma((8,)),
        ],
        compiler_params=pltpu.CompilerParams(
            collective_id=2, has_side_effects=True, vmem_limit_bytes=60 * 1024 * 1024
        ),
        name="reduce_rows",
    )(masked, local_numbers, weights, resid)


def per_device(feature_codes, block_ids, target_layer, request_ids, target_resid, decoder, grid=False):
    layers_here, count, kact, panel = feature_codes.shape
    width = target_resid.shape[1]
    features = decoder.shape[1]
    per_dev = features // panel
    tok, lyr = lax.axis_index("tok"), lax.axis_index("lyr")
    lyr_count = lax.axis_size("lyr")
    layer_ids = lyr * layers_here + jnp.arange(layers_here, dtype=jnp.int32)
    alive = layer_ids[:, None] <= target_layer[None, :]
    masked = jnp.where(alive[:, :, None, None], feature_codes, jnp.zeros_like(feature_codes))
    numbers = jnp.concatenate(
        [jnp.moveaxis(block_ids, 1, 2).reshape(layers_here * kact, count), request_ids[None, :]], axis=0
    )
    weights = decoder.reshape(layers_here * features, width)
    rows = count // lyr_count
    resid = lax.dynamic_slice_in_dim(target_resid, lyr * rows, rows, 0)
    if grid:
        numbers = jnp.concatenate([numbers, jnp.zeros((8 - numbers.shape[0], count), jnp.int32)], axis=0)
        by_k = jnp.moveaxis(masked, 1, 2).reshape(layers_here * kact, count, panel)
        gradient, dense, all_numbers = reduce_rows(by_k, numbers, weights, resid)
        scores, totals = gather_rows(gradient, dense, weights, all_numbers, numbers, panel)
        scores = jnp.moveaxis(scores.reshape(layers_here, kact, count, panel), 1, 2)
        return (scores, totals.reshape(REQUESTS, layers_here, features))
    all_codes = lax.all_gather(masked, "tok", axis=1, tiled=True)
    numbers = lax.all_gather(numbers, "tok", axis=1, tiled=True)
    all_ids = jnp.moveaxis(numbers[:-1].reshape(layers_here, kact, -1), 1, 2)
    all_requests = numbers[-1]
    mine = tok * per_dev + jnp.arange(per_dev, dtype=jnp.int32)
    named = (all_ids[..., None] == mine).astype(jnp.bfloat16)
    dense = jnp.sum(all_codes[:, :, :, None, :] * named[..., None], axis=2)
    tokens = dense.shape[1]
    dense = jnp.swapaxes(dense, 0, 1).reshape(tokens, layers_here * features)
    partial = jnp.dot(dense, weights, preferred_element_type=jnp.float32).astype(jnp.bfloat16)
    rebuilt = lax.psum_scatter(partial, ("tok", "lyr"), scatter_dimension=0, tiled=True)
    error = resid.astype(jnp.float32) - rebuilt.astype(jnp.float32)
    spread = jnp.mean(error * error, axis=-1, keepdims=True)
    gradient = (error * lax.rsqrt(spread + 1e-06)).astype(jnp.bfloat16)
    gradients = lax.all_gather(gradient, ("tok", "lyr"), axis=0, tiled=True)
    projected = lax.dot_general(
        gradients, weights, (((1,), (1,)), ((), ())), preferred_element_type=jnp.float32
    ).astype(jnp.bfloat16)
    attribution = dense.astype(jnp.float32) * projected.astype(jnp.float32)
    members = (all_requests[:, None] == jnp.arange(REQUESTS, dtype=jnp.int32)).astype(jnp.float32)
    totals = lax.dot_general(
        members, attribution, (((0,), (0,)), ((), ())), precision=lax.Precision.HIGHEST
    ).reshape(REQUESTS, layers_here, features)
    scored = attribution.astype(jnp.bfloat16).reshape(tokens, layers_here, 1, per_dev, panel)
    spread_out = jnp.sum(
        scored * jnp.swapaxes(named, 0, 1)[..., None], axis=3
    )
    scores = lax.psum_scatter(
        jnp.swapaxes(spread_out, 0, 1), "tok", scatter_dimension=1, tiled=True
    )
    return (scores, totals)


def solution(mesh):
    placed = (
        P("lyr", "tok", None, None),
        P("lyr", "tok", None),
        P("tok"),
        P("tok"),
        P("tok", None),
        P("lyr", "tok", None),
    )
    wide = len({getattr(d, "coords", (0,))[0] for d in mesh.devices.flat})
    grid = (mesh.shape["tok"], mesh.shape["lyr"]) == (16, 2) and wide == 2
    return jax.shard_map(
        functools.partial(per_device, grid=grid),
        mesh=mesh,
        in_specs=placed,
        out_specs=(P("lyr", "tok", None, None), P(None, "lyr", "tok")),
        check_vma=False,
    )
```

```python
import functools

import jax
import jax.numpy as jnp
from jax import lax
from jax.experimental import pallas as pl
from jax.experimental.pallas import tpu as pltpu
from jax.sharding import PartitionSpec as P

REQUESTS = 16
CAP = 16
MESH = pl.DeviceIdType.MESH


class Place:
    def __init__(self):
        tok, y = lax.axis_index("tok"), lax.axis_index("lyr")
        z, x, c = tok // 4, (tok // 2) % 2, tok % 2
        self.z, self.c = z, c
        self.inner = (z % 3) != 0
        self.first = (1 - c) * y + c * x
        self.second = (1 - c) * x + c * y
        across_x, across_y = (tok + 2 - 4 * x, y), (tok, 1 - y)
        self.to_first = tuple((1 - c) * a + c * b for a, b in zip(across_y, across_x))
        self.to_second = tuple((1 - c) * a + c * b for a, b in zip(across_x, across_y))
        self.to_core = (tok + 1 - 2 * c, y)
        self.tok, self.y = tok, y
        half = z // 2
        self.near = [z, z + 1 - 2 * (z % 2), 2 - half, 3 - 3 * half]

    def along(self, step):
        return (self.tok + 4 * step, self.y)

    def quarter(self, first, second):
        return (1 - self.c) * (second * 2 + first) + self.c * (first * 2 + second)

    def peer(self, distance):
        return ((self.tok + distance) % 16, self.y)

    def barrier(self):
        gate = pltpu.get_barrier_semaphore()
        for distance in range(1, 16):
            pl.semaphore_signal(gate, inc=1, device_id=self.peer(distance), device_id_type=MESH)
        pl.semaphore_signal(gate, inc=1, device_id=(self.tok, 1 - self.y), device_id_type=MESH)
        pl.semaphore_wait(gate, 16)


def earlier(count):
    shape = (count, count)
    return (lax.broadcasted_iota(jnp.int32, shape, 0) < lax.broadcasted_iota(jnp.int32, shape, 1)).astype(jnp.bfloat16)


def slots(numbers, layer, first_panel, panels):
    shape = (panels * CAP, numbers.shape[1])
    row = lax.broadcasted_iota(jnp.int32, shape, 0)
    panel = row // CAP + first_panel
    rank = (row % CAP).astype(jnp.float32)
    named = [numbers[2 * layer + k : 2 * layer + k + 1] == panel for k in (0, 1)]
    either = jnp.where(named[0] | named[1], 1.0, 0.0).astype(jnp.bfloat16)
    before = jnp.dot(either, earlier(shape[1]), preferred_element_type=jnp.float32)
    here = before == rank
    return [jnp.where(n & here, 1.0, 0.0).astype(jnp.bfloat16) for n in named]


def remote(src, dst, send, recv, target):
    return pltpu.make_async_remote_copy(
        src_ref=src, dst_ref=dst, send_sem=send, recv_sem=recv, device_id=target, device_id_type=MESH
    )


def gather_kernel(
    own_ref, dense_ref, weights_ref, numbers_ref, hot_ref, sent_ref, scores_ref, totals_ref,
    out_ref, slot_out, slot_in, local_sem, recv_sem, core_sem, first_sem, second_sem, z_sem, slot_send, slot_recv,
):
    at = Place()
    at.barrier()

    def block(z, first, second, core):
        return (z * 2 + core) * 4 + at.quarter(first, second)

    def mine(j, flip_first, flip_second):
        f = 1 - at.first if flip_first else at.first
        s = 1 - at.second if flip_second else at.second
        return block(at.near[j], f, s, at.c)

    def send(b, sem, target):
        remote(out_ref.at[b], out_ref.at[b], sem, recv_sem.at[b], target).start()

    def arrived(b):
        remote(out_ref.at[b], out_ref.at[b], core_sem.at[0], recv_sem.at[b], at.to_core).wait_recv()

    b0 = mine(0, False, False)
    keep = pltpu.make_async_copy(own_ref, out_ref.at[b0], local_sem)
    keep.start()
    keep.wait()
    used = [0, 0, 0]

    def fan(b, second, first):
        if second:
            send(b, second_sem.at[used[1]], at.to_second)
            used[1] += 1
        if first:
            send(b, first_sem.at[used[0]], at.to_first)
            used[0] += 1
        send(b, core_sem.at[used[2]], at.to_core)
        used[2] += 1

    @pl.when(at.z > 0)
    def _():
        send(b0, z_sem.at[0], at.along(-1))

    @pl.when(at.z < 3)
    def _():
        send(b0, z_sem.at[1], at.along(1))

    fan(b0, True, True)

    def from_z(j):
        b = mine(j, False, False)
        arrived(b)
        step = (3 - 2 * at.z) if j == 1 else (2 * at.z - 3)

        @pl.when(at.inner)
        def _():
            send(b, z_sem.at[1 + j], at.along(step))

        fan(b, True, True)

    def from_second(j):
        b = mine(j, False, True)
        arrived(b)
        fan(b, False, True)

    def from_first(j, flip):
        b = mine(j, True, flip)
        arrived(b)
        fan(b, False, False)

    rows = out_ref.shape[1]
    panel = slot_out.shape[-1]
    totals_ref[...] = jnp.zeros_like(totals_ref)

    def slot_copy(source):
        return remote(
            slot_out.at[source], slot_in.at[at.tok], slot_send.at[source], slot_recv.at[at.tok], (source, at.y)
        )

    def project(z, core, own):
        group = z * 2 + core
        left = out_ref[pl.ds(group * 4, 4)].reshape(4 * rows, out_ref.shape[2])
        sources = [(z * 2 + x) * 2 + core for x in (0, 1)]
        numbers = [numbers_ref[source] for source in sources]
        members = []
        for x in (0, 1):
            wanted = lax.broadcasted_iota(jnp.int32, (REQUESTS, 2 * rows), 0)
            members.append(jnp.where(numbers[x][4:5] == wanted, 1.0, 0.0).astype(jnp.bfloat16))
        for n in range(4):
            layer, which = n // 2, n % 2
            cols = slice(n * panel, (n + 1) * panel)
            product = lax.dot_general(
                left, weights_ref[cols, :], (((1,), (1,)), ((), ())), preferred_element_type=jnp.float32
            ).astype(jnp.bfloat16)
            for x in (0, 1):
                span = slice(x * 2 * rows, (x + 1) * 2 * rows)
                value = product[span].astype(jnp.float32) * dense_ref[group, x, :, cols].astype(jnp.float32)
                high = value.astype(jnp.bfloat16)
                low = (value - high.astype(jnp.float32)).astype(jnp.bfloat16)
                totals_ref[:, cols] += jnp.dot(members[x], high, preferred_element_type=jnp.float32) + jnp.dot(
                    members[x], low, preferred_element_type=jnp.float32
                )
                hot = hot_ref[sources[x], layer, which * CAP : (which + 1) * CAP, :]
                packed = jnp.dot(hot, high, preferred_element_type=jnp.float32).astype(jnp.bfloat16)
                slot_out[sources[x], layer, which * CAP : (which + 1) * CAP, :] = packed
        for x in (0, 1):
            if own:

                @pl.when(sources[x] != at.tok)
                def _():
                    slot_copy(sources[x]).start()

            else:
                slot_copy(sources[x]).start()

    def from_core(j):
        for q in range(4):
            arrived((at.near[j] * 2 + 1 - at.c) * 4 + q)
        project(at.near[j], 1 - at.c, False)

    from_second(0)
    from_z(1)
    from_first(0, False)
    from_second(1)
    from_z(2)
    from_first(0, True)
    from_first(1, False)
    from_second(2)
    from_z(3)
    from_first(1, True)
    project(at.near[0], at.c, True)
    from_first(2, False)
    from_second(3)
    from_core(0)
    project(at.near[1], at.c, False)
    from_first(2, True)
    project(at.near[2], at.c, False)
    from_first(3, False)
    from_core(1)
    from_first(3, True)
    from_core(2)
    project(at.near[3], at.c, False)
    from_core(3)
    slot_in[at.tok] = slot_out[at.tok]
    for distance in range(1, 16):
        source = (at.tok + distance) % 16
        remote(
            slot_out.at[0], slot_in.at[source], slot_send.at[0], slot_recv.at[source], at.to_core
        ).wait_recv()
    for layer in (0, 1):
        table = slot_in[:, layer].reshape(32 * CAP, panel)
        for k in (0, 1):
            scores_ref[2 * layer + k] = lax.dot_general(
                sent_ref[2 * layer + k], table, (((0,), (0,)), ((), ())), preferred_element_type=jnp.float32
            ).astype(scores_ref.dtype)
    for distance in range(1, 16):
        source = (at.tok + distance) % 16
        remote(
            slot_out.at[0], slot_in.at[0], slot_send.at[source], slot_recv.at[0], at.to_core
        ).wait_send()
    for i in range(16):
        remote(own_ref, own_ref, core_sem.at[i], recv_sem.at[0], at.to_core).wait_send()
    for i in range(8):
        remote(own_ref, own_ref, first_sem.at[i], recv_sem.at[0], at.to_core).wait_send()
    for i in range(4):
        remote(own_ref, own_ref, second_sem.at[i], recv_sem.at[0], at.to_core).wait_send()

    @pl.when(at.z > 0)
    def _():
        remote(own_ref, own_ref, z_sem.at[0], recv_sem.at[0], at.to_core).wait_send()

    @pl.when(at.z < 3)
    def _():
        remote(own_ref, own_ref, z_sem.at[1], recv_sem.at[0], at.to_core).wait_send()

    @pl.when(at.inner)
    def _():
        for i in range(2, 5):
            remote(own_ref, own_ref, z_sem.at[i], recv_sem.at[0], at.to_core).wait_send()


def gather_rows(own, dense, weights, numbers, hot, sent, panel):
    rows, width = own.shape
    dma, bf16 = pltpu.SemaphoreType.DMA, jnp.bfloat16
    vmem = pl.BlockSpec(memory_space=pltpu.VMEM)
    return pl.pallas_call(
        gather_kernel,
        out_shape=(
            jax.ShapeDtypeStruct((4, 2 * rows, panel), bf16),
            jax.ShapeDtypeStruct((REQUESTS, weights.shape[0]), jnp.float32),
        ),
        in_specs=[vmem] * 6,
        out_specs=(vmem, vmem),
        scratch_shapes=[
            pltpu.VMEM((32, rows, width), bf16),
            pltpu.VMEM((16, 2, 2 * CAP, panel), bf16),
            pltpu.VMEM((16, 2, 2 * CAP, panel), bf16),
            dma, dma((32,)), dma((16,)), dma((8,)), dma((4,)), dma((5,)), dma((16,)), dma((16,)),
        ],
        compiler_params=pltpu.CompilerParams(
            collective_id=1, has_side_effects=True, vmem_limit_bytes=60 * 1024 * 1024
        ),
        name="gather_rows",
    )(own, dense, weights, numbers, hot, sent)


def reduce_kernel(
    masked_ref, local_numbers_ref, weights_ref, resid_ref,
    out_ref, codes_ref, numbers_ref, hot_ref, sent_ref,
    packed, slot_in, slot_send, slot_recv, number_send, number_recv, held, core_out, core_in, first_out, first_in, second_out, second_in, z_out, z_in,
    core_send, core_recv, first_send, first_recv, second_send, second_recv, z_send, z_recv,
):
    at = Place()
    at.barrier()
    rows, width = out_ref.shape
    depth = codes_ref.shape[-1]
    panel = packed.shape[-1]
    far = at.near[::-1]
    local = local_numbers_ref[...]
    numbers_ref[at.tok] = local
    for layer in (0, 1):
        sent = slots(local, layer, 0, 32)
        for k in (0, 1):
            sent_ref[2 * layer + k] = sent[k]
        value = sum(
            jnp.dot(sent[k], masked_ref[2 * layer + k], preferred_element_type=jnp.float32) for k in (0, 1)
        )
        packed[:, layer] = value.astype(packed.dtype).reshape(16, 2 * CAP, panel)

    def peers(i):
        return [far[i] * 4 + (at.tok + step) % 4 for step in range(1 if i == 3 else 0, 4)]

    def slot_copies(target, source):
        return (
            remote(packed.at[target], slot_in.at[source], slot_send.at[target], slot_recv.at[source], (target, at.y)),
            remote(
                local_numbers_ref, numbers_ref.at[source], number_send.at[target], number_recv.at[source],
                (target, at.y),
            ),
        )

    for i in range(4):
        for target in peers(i):
            for copy in slot_copies(target, at.tok):
                copy.start()
    slot_in[at.tok] = packed[at.tok]

    def unpack(i):
        for source in peers(i):
            for copy in slot_copies(source, source):
                copy.wait_recv()

        @pl.loop(0, 4)
        def _(step):
            source = far[i] * 4 + step
            for layer in (0, 1):
                held_slots = slots(numbers_ref[source], layer, at.tok * 2, 2)
                hot = held_slots[0] + held_slots[1]
                hot_ref[source, layer] = hot
                for which in (0, 1):
                    part = slice(which * CAP, (which + 1) * CAP)
                    n = 2 * layer + which
                    codes_ref[far[i] * 2 + step % 2, step // 2, :, n * panel : (n + 1) * panel] = (
                        lax.dot_general(
                            hot[part], slot_in[source, layer, part, :], (((0,), (0,)), ((), ())),
                            preferred_element_type=jnp.float32,
                        ).astype(codes_ref.dtype)
                    )

    tile = 256 if width % 256 == 0 else width

    def product(i):
        unpack(i)
        for core in (1 - at.c, at.c):
            left = codes_ref[far[i] * 2 + core].reshape(4 * rows, depth)
            away = core is not at.c

            @pl.loop(0, width // tile)
            def _(n):
                cols = pl.ds(pl.multiple_of(n * tile, tile), tile)
                value = jnp.dot(left, weights_ref[:, cols], preferred_element_type=jnp.float32)
                value = value.reshape(4, rows, tile)
                if away:
                    core_out[i, :, :, cols] = value.astype(core_out.dtype)
                else:
                    held[i, :, :, cols] = value

            if away:
                core_copy(i).start()

    def core_copy(i):
        return remote(core_out.at[i], core_in.at[i], core_send.at[i], core_recv.at[i], at.to_core)

    def first_copy(i, k):
        return remote(first_out.at[i, k], first_in.at[i, k], first_send.at[i, k], first_recv.at[i, k], at.to_first)

    def second_copy(i):
        return remote(second_out.at[i], second_in.at[i], second_send.at[i], second_recv.at[i], at.to_second)

    def z_copy(i, way, step):
        slot = way * 4 + far[i]
        return remote(z_out.at[i], z_in.at[slot], z_send.at[i], z_recv.at[slot], at.along(step))

    def f32(v):
        return v.astype(jnp.float32)

    def both(i, q):
        return held[i, q] + f32(core_in[i, q])

    def spot(k):
        return 1 - at.second if k == 0 else at.second

    def over_first(i):
        core_copy(i).wait_recv()
        for k in (0, 1):
            first_out[i, k] = both(i, at.quarter(1 - at.first, spot(k))).astype(first_out.dtype)
            first_copy(i, k).start()

    def over_second(i):
        first_copy(i, 0).wait_recv()
        total = both(i, at.quarter(at.first, spot(0))) + f32(first_in[i, 0])
        second_out[i] = total.astype(second_out.dtype)
        second_copy(i).start()

    def z_arrived(slot):
        remote(z_in.at[slot], z_in.at[slot], z_send.at[0], z_recv.at[slot], at.to_core).wait_recv()

    def along_z(i):
        first_copy(i, 1).wait_recv()
        second_copy(i).wait_recv()
        q = at.quarter(at.first, at.second)
        total = both(i, q) + f32(first_in[i, 1]) + f32(second_in[i])
        held[i, q] = total
        if i < 3:
            way = (at.z // 2) if i < 2 else (at.z % 2)
            slot = way * 4 + far[i]

            @pl.when(at.inner)
            def _():
                z_arrived(slot)
                z_out[i] = (held[i, q] + f32(z_in[slot])).astype(z_out.dtype)

            @pl.when(jnp.logical_not(at.inner))
            def _():
                z_out[i] = held[i, q].astype(z_out.dtype)

            z_copy(i, way, 1 - 2 * way).start()
        else:
            @pl.when(at.z > 0)
            def _():
                z_arrived(at.z)
                held[i, q] += f32(z_in[at.z])

            @pl.when(at.z < 3)
            def _():
                z_arrived(4 + at.z)
                held[i, q] += f32(z_in[4 + at.z])

            error = f32(resid_ref[...]) - held[i, q]
            spread = jnp.mean(error * error, axis=-1, keepdims=True)
            out_ref[...] = (error * lax.rsqrt(spread + 1e-06)).astype(out_ref.dtype)

    product(0)
    product(1)
    over_first(0)
    product(2)
    over_first(1)
    over_second(0)
    product(3)
    over_first(2)
    over_second(1)
    along_z(0)
    over_first(3)
    over_second(2)
    along_z(1)
    over_second(3)
    along_z(2)
    along_z(3)
    for i in range(4):
        for target in peers(i):
            for copy in slot_copies(target, target):
                copy.wait_send()
    for i in range(4):
        core_copy(i).wait_send()
        first_copy(i, 0).wait_send()
        first_copy(i, 1).wait_send()
        second_copy(i).wait_send()
        if i < 3:
            remote(z_out.at[i], z_out.at[i], z_send.at[i], z_recv.at[0], at.to_core).wait_send()


def reduce_rows(masked, local_numbers, weights, resid):
    rows, width = resid.shape
    depth = weights.shape[0]
    panel = masked.shape[-1]
    dma, bf16 = pltpu.SemaphoreType.DMA, jnp.bfloat16
    vmem = pl.BlockSpec(memory_space=pltpu.VMEM)
    block = (rows, width)
    return pl.pallas_call(
        reduce_kernel,
        out_shape=(
            jax.ShapeDtypeStruct(block, bf16),
            jax.ShapeDtypeStruct((8, 2, 2 * rows, depth), bf16),
            jax.ShapeDtypeStruct((16,) + local_numbers.shape, jnp.int32),
            jax.ShapeDtypeStruct((16, 2, 2 * CAP, 2 * rows), bf16),
            jax.ShapeDtypeStruct((4, 32 * CAP, 2 * rows), bf16),
        ),
        in_specs=[vmem] * 4,
        out_specs=(vmem,) * 5,
        scratch_shapes=[
            pltpu.VMEM((16, 2, 2 * CAP, panel), bf16),
            pltpu.VMEM((16, 2, 2 * CAP, panel), bf16),
            dma((16,)), dma((16,)), dma((16,)), dma((16,)),
            pltpu.VMEM((4, 4) + block, jnp.float32),
            pltpu.VMEM((4, 4) + block, bf16),
            pltpu.VMEM((4, 4) + block, bf16),
            pltpu.VMEM((4, 2) + block, bf16),
            pltpu.VMEM((4, 2) + block, bf16),
            pltpu.VMEM((4,) + block, bf16),
            pltpu.VMEM((4,) + block, bf16),
            pltpu.VMEM((3,) + block, bf16),
            pltpu.VMEM((8,) + block, bf16),
            dma((4,)), dma((4,)), dma((4, 2)), dma((4, 2)), dma((4,)), dma((4,)), dma((3,)), dma((8,)),
        ],
        compiler_params=pltpu.CompilerParams(
            collective_id=2, has_side_effects=True, vmem_limit_bytes=60 * 1024 * 1024
        ),
        name="reduce_rows",
    )(masked, local_numbers, weights, resid)


def per_device(feature_codes, block_ids, target_layer, request_ids, target_resid, decoder, grid=False):
    layers_here, count, kact, panel = feature_codes.shape
    width = target_resid.shape[1]
    features = decoder.shape[1]
    per_dev = features // panel
    tok, lyr = lax.axis_index("tok"), lax.axis_index("lyr")
    lyr_count = lax.axis_size("lyr")
    layer_ids = lyr * layers_here + jnp.arange(layers_here, dtype=jnp.int32)
    alive = layer_ids[:, None] <= target_layer[None, :]
    masked = jnp.where(alive[:, :, None, None], feature_codes, jnp.zeros_like(feature_codes))
    numbers = jnp.concatenate(
        [jnp.moveaxis(block_ids, 1, 2).reshape(layers_here * kact, count), request_ids[None, :]], axis=0
    )
    weights = decoder.reshape(layers_here * features, width)
    rows = count // lyr_count
    resid = lax.dynamic_slice_in_dim(target_resid, lyr * rows, rows, 0)
    if grid:
        numbers = jnp.concatenate([numbers, jnp.zeros((8 - numbers.shape[0], count), jnp.int32)], axis=0)
        by_k = jnp.moveaxis(masked, 1, 2).reshape(layers_here * kact, count, panel)
        gradient, *rest = reduce_rows(by_k, numbers, weights, resid)
        dense, all_numbers, hot, sent = rest
        scores, totals = gather_rows(gradient, dense, weights, all_numbers, hot, sent, panel)
        scores = jnp.moveaxis(scores.reshape(layers_here, kact, count, panel), 1, 2)
        return (scores, totals.reshape(REQUESTS, layers_here, features))
    all_codes = lax.all_gather(masked, "tok", axis=1, tiled=True)
    numbers = lax.all_gather(numbers, "tok", axis=1, tiled=True)
    all_ids = jnp.moveaxis(numbers[:-1].reshape(layers_here, kact, -1), 1, 2)
    all_requests = numbers[-1]
    mine = tok * per_dev + jnp.arange(per_dev, dtype=jnp.int32)
    named = (all_ids[..., None] == mine).astype(jnp.bfloat16)
    dense = jnp.sum(all_codes[:, :, :, None, :] * named[..., None], axis=2)
    tokens = dense.shape[1]
    dense = jnp.swapaxes(dense, 0, 1).reshape(tokens, layers_here * features)
    partial = jnp.dot(dense, weights, preferred_element_type=jnp.float32).astype(jnp.bfloat16)
    rebuilt = lax.psum_scatter(partial, ("tok", "lyr"), scatter_dimension=0, tiled=True)
    error = resid.astype(jnp.float32) - rebuilt.astype(jnp.float32)
    spread = jnp.mean(error * error, axis=-1, keepdims=True)
    gradient = (error * lax.rsqrt(spread + 1e-06)).astype(jnp.bfloat16)
    gradients = lax.all_gather(gradient, ("tok", "lyr"), axis=0, tiled=True)
    projected = lax.dot_general(
        gradients, weights, (((1,), (1,)), ((), ())), preferred_element_type=jnp.float32
    ).astype(jnp.bfloat16)
    attribution = dense.astype(jnp.float32) * projected.astype(jnp.float32)
    members = (all_requests[:, None] == jnp.arange(REQUESTS, dtype=jnp.int32)).astype(jnp.float32)
    totals = lax.dot_general(
        members, attribution, (((0,), (0,)), ((), ())), precision=lax.Precision.HIGHEST
    ).reshape(REQUESTS, layers_here, features)
    scored = attribution.astype(jnp.bfloat16).reshape(tokens, layers_here, 1, per_dev, panel)
    spread_out = jnp.sum(
        scored * jnp.swapaxes(named, 0, 1)[..., None], axis=3
    )
    scores = lax.psum_scatter(
        jnp.swapaxes(spread_out, 0, 1), "tok", scatter_dimension=1, tiled=True
    )
    return (scores, totals)


def solution(mesh):
    placed = (
        P("lyr", "tok", None, None),
        P("lyr", "tok", None),
        P("tok"),
        P("tok"),
        P("tok", None),
        P("lyr", "tok", None),
    )
    wide = len({getattr(d, "coords", (0,))[0] for d in mesh.devices.flat})
    grid = (mesh.shape["tok"], mesh.shape["lyr"]) == (16, 2) and wide == 2
    return jax.shard_map(
        functools.partial(per_device, grid=grid),
        mesh=mesh,
        in_specs=placed,
        out_specs=(P("lyr", "tok", None, None), P(None, "lyr", "tok")),
        check_vma=False,
    )
```

```python
import functools

import jax
import jax.numpy as jnp
from jax import lax
from jax.experimental import pallas as pl
from jax.experimental.pallas import tpu as pltpu
from jax.sharding import PartitionSpec as P

REQUESTS = 16
CAP = 16
MESH = pl.DeviceIdType.MESH


class Place:
    def __init__(self):
        tok, y = lax.axis_index("tok"), lax.axis_index("lyr")
        z, x, c = tok // 4, (tok // 2) % 2, tok % 2
        self.z, self.c = z, c
        self.inner = (z % 3) != 0
        self.first = (1 - c) * y + c * x
        self.second = (1 - c) * x + c * y
        across_x, across_y = (tok + 2 - 4 * x, y), (tok, 1 - y)
        self.to_first = tuple((1 - c) * a + c * b for a, b in zip(across_y, across_x))
        self.to_second = tuple((1 - c) * a + c * b for a, b in zip(across_x, across_y))
        self.to_core = (tok + 1 - 2 * c, y)
        self.tok, self.y = tok, y
        half = z // 2
        self.near = [z, z + 1 - 2 * (z % 2), 2 - half, 3 - 3 * half]

    def along(self, step):
        return (self.tok + 4 * step, self.y)

    def quarter(self, first, second):
        return (1 - self.c) * (second * 2 + first) + self.c * (first * 2 + second)

    def peer(self, distance):
        return ((self.tok + distance) % 16, self.y)

    def barrier(self):
        gate = pltpu.get_barrier_semaphore()
        for distance in range(1, 16):
            pl.semaphore_signal(gate, inc=1, device_id=self.peer(distance), device_id_type=MESH)
        pl.semaphore_signal(gate, inc=1, device_id=(self.tok, 1 - self.y), device_id_type=MESH)
        pl.semaphore_wait(gate, 16)


def earlier(count):
    shape = (count, count)
    return (lax.broadcasted_iota(jnp.int32, shape, 0) < lax.broadcasted_iota(jnp.int32, shape, 1)).astype(jnp.bfloat16)


def slots(numbers, layer, first_panel, panels):
    shape = (panels * CAP, numbers.shape[1])
    row = lax.broadcasted_iota(jnp.int32, shape, 0)
    panel = row // CAP + first_panel
    rank = (row % CAP).astype(jnp.float32)
    named = [numbers[2 * layer + k : 2 * layer + k + 1] == panel for k in (0, 1)]
    either = jnp.where(named[0] | named[1], 1.0, 0.0).astype(jnp.bfloat16)
    before = jnp.dot(either, earlier(shape[1]), preferred_element_type=jnp.float32)
    here = before == rank
    return [jnp.where(n & here, 1.0, 0.0).astype(jnp.bfloat16) for n in named]


def remote(src, dst, send, recv, target):
    return pltpu.make_async_remote_copy(
        src_ref=src, dst_ref=dst, send_sem=send, recv_sem=recv, device_id=target, device_id_type=MESH
    )


def gather_kernel(
    own_ref, dense_ref, weights_ref, numbers_ref, hot_ref, sent_ref, scores_ref, totals_ref,
    out_ref, slot_out, slot_in, local_sem, recv_sem, core_sem, first_sem, second_sem, z_sem, slot_send, slot_recv,
):
    at = Place()
    at.barrier()

    def block(z, first, second, core):
        return (z * 2 + core) * 4 + at.quarter(first, second)

    def mine(j, flip_first, flip_second):
        f = 1 - at.first if flip_first else at.first
        s = 1 - at.second if flip_second else at.second
        return block(at.near[j], f, s, at.c)

    def send(b, sem, target):
        remote(out_ref.at[b], out_ref.at[b], sem, recv_sem.at[b], target).start()

    def arrived(b):
        remote(out_ref.at[b], out_ref.at[b], core_sem.at[0], recv_sem.at[b], at.to_core).wait_recv()

    b0 = mine(0, False, False)
    keep = pltpu.make_async_copy(own_ref, out_ref.at[b0], local_sem)
    keep.start()
    keep.wait()
    used = [0, 0, 0]

    def fan(b, second, first):
        if second:
            send(b, second_sem.at[used[1]], at.to_second)
            used[1] += 1
        if first:
            send(b, first_sem.at[used[0]], at.to_first)
            used[0] += 1
        send(b, core_sem.at[used[2]], at.to_core)
        used[2] += 1

    @pl.when(at.z > 0)
    def _():
        send(b0, z_sem.at[0], at.along(-1))

    @pl.when(at.z < 3)
    def _():
        send(b0, z_sem.at[1], at.along(1))

    fan(b0, True, True)

    def from_z(j):
        b = mine(j, False, False)
        arrived(b)
        step = (3 - 2 * at.z) if j == 1 else (2 * at.z - 3)

        @pl.when(at.inner)
        def _():
            send(b, z_sem.at[1 + j], at.along(step))

        fan(b, True, True)

    def from_second(j):
        b = mine(j, False, True)
        arrived(b)
        fan(b, False, True)

    def from_first(j, flip):
        b = mine(j, True, flip)
        arrived(b)
        fan(b, False, False)

    rows = out_ref.shape[1]
    panel = slot_out.shape[-1]
    totals_ref[...] = jnp.zeros_like(totals_ref)

    def slot_copy(source):
        return remote(
            slot_out.at[source], slot_in.at[at.tok], slot_send.at[source], slot_recv.at[at.tok], (source, at.y)
        )

    def project(z, core, own):
        group = z * 2 + core
        left = out_ref[pl.ds(group * 4, 4)].reshape(4 * rows, out_ref.shape[2])
        sources = [(z * 2 + x) * 2 + core for x in (0, 1)]
        numbers = [numbers_ref[source] for source in sources]
        members = []
        for x in (0, 1):
            wanted = lax.broadcasted_iota(jnp.int32, (REQUESTS, 2 * rows), 0)
            members.append(jnp.where(numbers[x][4:5] == wanted, 1.0, 0.0).astype(jnp.bfloat16))
        for n in range(4):
            layer, which = n // 2, n % 2
            cols = slice(n * panel, (n + 1) * panel)
            product = lax.dot_general(
                left, weights_ref[cols, :], (((1,), (1,)), ((), ())), preferred_element_type=jnp.float32
            ).astype(jnp.bfloat16)
            for x in (0, 1):
                span = slice(x * 2 * rows, (x + 1) * 2 * rows)
                value = product[span].astype(jnp.float32) * dense_ref[group, x, :, cols].astype(jnp.float32)
                high = value.astype(jnp.bfloat16)
                low = (value - high.astype(jnp.float32)).astype(jnp.bfloat16)
                totals_ref[:, cols] += jnp.dot(members[x], high, preferred_element_type=jnp.float32) + jnp.dot(
                    members[x], low, preferred_element_type=jnp.float32
                )
                hot = hot_ref[sources[x], layer, which * CAP : (which + 1) * CAP, :]
                packed = jnp.dot(hot, high, preferred_element_type=jnp.float32).astype(jnp.bfloat16)
                slot_out[sources[x], layer, which * CAP : (which + 1) * CAP, :] = packed
        for x in (0, 1):
            if own:

                @pl.when(sources[x] != at.tok)
                def _():
                    slot_copy(sources[x]).start()

            else:
                slot_copy(sources[x]).start()

    def from_core(j):
        for q in range(4):
            arrived((at.near[j] * 2 + 1 - at.c) * 4 + q)
        project(at.near[j], 1 - at.c, False)

    from_second(0)
    from_z(1)
    from_first(0, False)
    from_second(1)
    from_z(2)
    from_first(0, True)
    from_first(1, False)
    from_second(2)
    from_z(3)
    from_first(1, True)
    from_first(2, False)
    from_second(3)
    project(at.near[0], at.c, True)
    from_core(0)
    project(at.near[1], at.c, False)
    from_first(2, True)
    project(at.near[2], at.c, False)
    from_first(3, False)
    from_core(1)
    from_first(3, True)
    from_core(2)
    project(at.near[3], at.c, False)
    from_core(3)
    slot_in[at.tok] = slot_out[at.tok]
    for distance in range(1, 16):
        source = (at.tok + distance) % 16
        remote(
            slot_out.at[0], slot_in.at[source], slot_send.at[0], slot_recv.at[source], at.to_core
        ).wait_recv()
    for layer in (0, 1):
        table = slot_in[:, layer].reshape(32 * CAP, panel)
        for k in (0, 1):
            scores_ref[2 * layer + k] = lax.dot_general(
                sent_ref[2 * layer + k], table, (((0,), (0,)), ((), ())), preferred_element_type=jnp.float32
            ).astype(scores_ref.dtype)
    for distance in range(1, 16):
        source = (at.tok + distance) % 16
        remote(
            slot_out.at[0], slot_in.at[0], slot_send.at[source], slot_recv.at[0], at.to_core
        ).wait_send()
    for i in range(16):
        remote(own_ref, own_ref, core_sem.at[i], recv_sem.at[0], at.to_core).wait_send()
    for i in range(8):
        remote(own_ref, own_ref, first_sem.at[i], recv_sem.at[0], at.to_core).wait_send()
    for i in range(4):
        remote(own_ref, own_ref, second_sem.at[i], recv_sem.at[0], at.to_core).wait_send()

    @pl.when(at.z > 0)
    def _():
        remote(own_ref, own_ref, z_sem.at[0], recv_sem.at[0], at.to_core).wait_send()

    @pl.when(at.z < 3)
    def _():
        remote(own_ref, own_ref, z_sem.at[1], recv_sem.at[0], at.to_core).wait_send()

    @pl.when(at.inner)
    def _():
        for i in range(2, 5):
            remote(own_ref, own_ref, z_sem.at[i], recv_sem.at[0], at.to_core).wait_send()


def gather_rows(own, dense, weights, numbers, hot, sent, panel):
    rows, width = own.shape
    dma, bf16 = pltpu.SemaphoreType.DMA, jnp.bfloat16
    vmem = pl.BlockSpec(memory_space=pltpu.VMEM)
    return pl.pallas_call(
        gather_kernel,
        out_shape=(
            jax.ShapeDtypeStruct((4, 2 * rows, panel), bf16),
            jax.ShapeDtypeStruct((REQUESTS, weights.shape[0]), jnp.float32),
        ),
        in_specs=[vmem] * 6,
        out_specs=(vmem, vmem),
        scratch_shapes=[
            pltpu.VMEM((32, rows, width), bf16),
            pltpu.VMEM((16, 2, 2 * CAP, panel), bf16),
            pltpu.VMEM((16, 2, 2 * CAP, panel), bf16),
            dma, dma((32,)), dma((16,)), dma((8,)), dma((4,)), dma((5,)), dma((16,)), dma((16,)),
        ],
        compiler_params=pltpu.CompilerParams(
            collective_id=1, has_side_effects=True, vmem_limit_bytes=60 * 1024 * 1024
        ),
        name="gather_rows",
    )(own, dense, weights, numbers, hot, sent)


def reduce_kernel(
    masked_ref, local_numbers_ref, weights_ref, resid_ref,
    out_ref, codes_ref, numbers_ref, hot_ref, sent_ref,
    packed, slot_in, slot_send, slot_recv, number_send, number_recv, held, core_out, core_in, first_out, first_in, second_out, second_in, z_out, z_in,
    core_send, core_recv, first_send, first_recv, second_send, second_recv, z_send, z_recv,
):
    at = Place()
    at.barrier()
    rows, width = out_ref.shape
    depth = codes_ref.shape[-1]
    panel = packed.shape[-1]
    far = at.near[::-1]
    local = local_numbers_ref[...]
    numbers_ref[at.tok] = local
    for layer in (0, 1):
        sent = slots(local, layer, 0, 32)
        for k in (0, 1):
            sent_ref[2 * layer + k] = sent[k]
        value = sum(
            jnp.dot(sent[k], masked_ref[2 * layer + k], preferred_element_type=jnp.float32) for k in (0, 1)
        )
        packed[:, layer] = value.astype(packed.dtype).reshape(16, 2 * CAP, panel)

    def peers(i):
        return [far[i] * 4 + (at.tok + step) % 4 for step in range(1 if i == 3 else 0, 4)]

    def slot_copies(target, source):
        return (
            remote(packed.at[target], slot_in.at[source], slot_send.at[target], slot_recv.at[source], (target, at.y)),
            remote(
                local_numbers_ref, numbers_ref.at[source], number_send.at[target], number_recv.at[source],
                (target, at.y),
            ),
        )

    for i in range(4):
        for target in peers(i):
            for copy in slot_copies(target, at.tok):
                copy.start()
    slot_in[at.tok] = packed[at.tok]

    def unpack(i):
        for source in peers(i):
            for copy in slot_copies(source, source):
                copy.wait_recv()

        @pl.loop(0, 4)
        def _(step):
            source = far[i] * 4 + step
            for layer in (0, 1):
                held_slots = slots(numbers_ref[source], layer, at.tok * 2, 2)
                hot = held_slots[0] + held_slots[1]
                hot_ref[source, layer] = hot
                for which in (0, 1):
                    part = slice(which * CAP, (which + 1) * CAP)
                    n = 2 * layer + which
                    codes_ref[far[i] * 2 + step % 2, step // 2, :, n * panel : (n + 1) * panel] = (
                        lax.dot_general(
                            hot[part], slot_in[source, layer, part, :], (((0,), (0,)), ((), ())),
                            preferred_element_type=jnp.float32,
                        ).astype(codes_ref.dtype)
                    )

    tile = 256 if width % 256 == 0 else width

    def product(i):
        unpack(i)
        for core in (1 - at.c, at.c):
            left = codes_ref[far[i] * 2 + core].reshape(4 * rows, depth)
            away = core is not at.c

            @pl.loop(0, width // tile)
            def _(n):
                cols = pl.ds(pl.multiple_of(n * tile, tile), tile)
                value = jnp.dot(left, weights_ref[:, cols], preferred_element_type=jnp.float32)
                value = value.reshape(4, rows, tile)
                if away:
                    core_out[i, :, :, cols] = value.astype(core_out.dtype)
                else:
                    held[i, :, :, cols] = value

            if away:
                core_copy(i).start()

    def core_copy(i):
        return remote(core_out.at[i], core_in.at[i], core_send.at[i], core_recv.at[i], at.to_core)

    def first_copy(i, k):
        return remote(first_out.at[i, k], first_in.at[i, k], first_send.at[i, k], first_recv.at[i, k], at.to_first)

    def second_copy(i):
        return remote(second_out.at[i], second_in.at[i], second_send.at[i], second_recv.at[i], at.to_second)

    def z_copy(i, way, step):
        slot = way * 4 + far[i]
        return remote(z_out.at[i], z_in.at[slot], z_send.at[i], z_recv.at[slot], at.along(step))

    def f32(v):
        return v.astype(jnp.float32)

    def both(i, q):
        return held[i, q] + f32(core_in[i, q])

    def spot(k):
        return 1 - at.second if k == 0 else at.second

    def over_first(i):
        core_copy(i).wait_recv()
        for k in (0, 1):
            first_out[i, k] = both(i, at.quarter(1 - at.first, spot(k))).astype(first_out.dtype)
            first_copy(i, k).start()

    def over_second(i):
        first_copy(i, 0).wait_recv()
        total = both(i, at.quarter(at.first, spot(0))) + f32(first_in[i, 0])
        second_out[i] = total.astype(second_out.dtype)
        second_copy(i).start()

    def z_arrived(slot):
        remote(z_in.at[slot], z_in.at[slot], z_send.at[0], z_recv.at[slot], at.to_core).wait_recv()

    def along_z(i):
        first_copy(i, 1).wait_recv()
        second_copy(i).wait_recv()
        q = at.quarter(at.first, at.second)
        total = both(i, q) + f32(first_in[i, 1]) + f32(second_in[i])
        held[i, q] = total
        if i < 3:
            way = (at.z // 2) if i < 2 else (at.z % 2)
            slot = way * 4 + far[i]

            @pl.when(at.inner)
            def _():
                z_arrived(slot)
                z_out[i] = (held[i, q] + f32(z_in[slot])).astype(z_out.dtype)

            @pl.when(jnp.logical_not(at.inner))
            def _():
                z_out[i] = held[i, q].astype(z_out.dtype)

            z_copy(i, way, 1 - 2 * way).start()
        else:
            @pl.when(at.z > 0)
            def _():
                z_arrived(at.z)
                held[i, q] += f32(z_in[at.z])

            @pl.when(at.z < 3)
            def _():
                z_arrived(4 + at.z)
                held[i, q] += f32(z_in[4 + at.z])

            error = f32(resid_ref[...]) - held[i, q]
            spread = jnp.mean(error * error, axis=-1, keepdims=True)
            out_ref[...] = (error * lax.rsqrt(spread + 1e-06)).astype(out_ref.dtype)

    product(0)
    over_first(0)
    product(1)
    over_first(1)
    over_second(0)
    product(2)
    over_first(2)
    over_second(1)
    along_z(0)
    product(3)
    over_first(3)
    over_second(2)
    along_z(1)
    over_second(3)
    along_z(2)
    along_z(3)
    for i in range(4):
        for target in peers(i):
            for copy in slot_copies(target, target):
                copy.wait_send()
    for i in range(4):
        core_copy(i).wait_send()
        first_copy(i, 0).wait_send()
        first_copy(i, 1).wait_send()
        second_copy(i).wait_send()
        if i < 3:
            remote(z_out.at[i], z_out.at[i], z_send.at[i], z_recv.at[0], at.to_core).wait_send()


def reduce_rows(masked, local_numbers, weights, resid):
    rows, width = resid.shape
    depth = weights.shape[0]
    panel = masked.shape[-1]
    dma, bf16 = pltpu.SemaphoreType.DMA, jnp.bfloat16
    vmem = pl.BlockSpec(memory_space=pltpu.VMEM)
    block = (rows, width)
    return pl.pallas_call(
        reduce_kernel,
        out_shape=(
            jax.ShapeDtypeStruct(block, bf16),
            jax.ShapeDtypeStruct((8, 2, 2 * rows, depth), bf16),
            jax.ShapeDtypeStruct((16,) + local_numbers.shape, jnp.int32),
            jax.ShapeDtypeStruct((16, 2, 2 * CAP, 2 * rows), bf16),
            jax.ShapeDtypeStruct((4, 32 * CAP, 2 * rows), bf16),
        ),
        in_specs=[vmem] * 4,
        out_specs=(vmem,) * 5,
        scratch_shapes=[
            pltpu.VMEM((16, 2, 2 * CAP, panel), bf16),
            pltpu.VMEM((16, 2, 2 * CAP, panel), bf16),
            dma((16,)), dma((16,)), dma((16,)), dma((16,)),
            pltpu.VMEM((4, 4) + block, jnp.float32),
            pltpu.VMEM((4, 4) + block, bf16),
            pltpu.VMEM((4, 4) + block, bf16),
            pltpu.VMEM((4, 2) + block, bf16),
            pltpu.VMEM((4, 2) + block, bf16),
            pltpu.VMEM((4,) + block, bf16),
            pltpu.VMEM((4,) + block, bf16),
            pltpu.VMEM((3,) + block, bf16),
            pltpu.VMEM((8,) + block, bf16),
            dma((4,)), dma((4,)), dma((4, 2)), dma((4, 2)), dma((4,)), dma((4,)), dma((3,)), dma((8,)),
        ],
        compiler_params=pltpu.CompilerParams(
            collective_id=2, has_side_effects=True, vmem_limit_bytes=60 * 1024 * 1024
        ),
        name="reduce_rows",
    )(masked, local_numbers, weights, resid)


def per_device(feature_codes, block_ids, target_layer, request_ids, target_resid, decoder, grid=False):
    layers_here, count, kact, panel = feature_codes.shape
    width = target_resid.shape[1]
    features = decoder.shape[1]
    per_dev = features // panel
    tok, lyr = lax.axis_index("tok"), lax.axis_index("lyr")
    lyr_count = lax.axis_size("lyr")
    layer_ids = lyr * layers_here + jnp.arange(layers_here, dtype=jnp.int32)
    alive = layer_ids[:, None] <= target_layer[None, :]
    masked = jnp.where(alive[:, :, None, None], feature_codes, jnp.zeros_like(feature_codes))
    numbers = jnp.concatenate(
        [jnp.moveaxis(block_ids, 1, 2).reshape(layers_here * kact, count), request_ids[None, :]], axis=0
    )
    weights = decoder.reshape(layers_here * features, width)
    rows = count // lyr_count
    resid = lax.dynamic_slice_in_dim(target_resid, lyr * rows, rows, 0)
    if grid:
        numbers = jnp.concatenate([numbers, jnp.zeros((8 - numbers.shape[0], count), jnp.int32)], axis=0)
        by_k = jnp.moveaxis(masked, 1, 2).reshape(layers_here * kact, count, panel)
        gradient, *rest = reduce_rows(by_k, numbers, weights, resid)
        dense, all_numbers, hot, sent = rest
        scores, totals = gather_rows(gradient, dense, weights, all_numbers, hot, sent, panel)
        scores = jnp.moveaxis(scores.reshape(layers_here, kact, count, panel), 1, 2)
        return (scores, totals.reshape(REQUESTS, layers_here, features))
    all_codes = lax.all_gather(masked, "tok", axis=1, tiled=True)
    numbers = lax.all_gather(numbers, "tok", axis=1, tiled=True)
    all_ids = jnp.moveaxis(numbers[:-1].reshape(layers_here, kact, -1), 1, 2)
    all_requests = numbers[-1]
    mine = tok * per_dev + jnp.arange(per_dev, dtype=jnp.int32)
    named = (all_ids[..., None] == mine).astype(jnp.bfloat16)
    dense = jnp.sum(all_codes[:, :, :, None, :] * named[..., None], axis=2)
    tokens = dense.shape[1]
    dense = jnp.swapaxes(dense, 0, 1).reshape(tokens, layers_here * features)
    partial = jnp.dot(dense, weights, preferred_element_type=jnp.float32).astype(jnp.bfloat16)
    rebuilt = lax.psum_scatter(partial, ("tok", "lyr"), scatter_dimension=0, tiled=True)
    error = resid.astype(jnp.float32) - rebuilt.astype(jnp.float32)
    spread = jnp.mean(error * error, axis=-1, keepdims=True)
    gradient = (error * lax.rsqrt(spread + 1e-06)).astype(jnp.bfloat16)
    gradients = lax.all_gather(gradient, ("tok", "lyr"), axis=0, tiled=True)
    projected = lax.dot_general(
        gradients, weights, (((1,), (1,)), ((), ())), preferred_element_type=jnp.float32
    ).astype(jnp.bfloat16)
    attribution = dense.astype(jnp.float32) * projected.astype(jnp.float32)
    members = (all_requests[:, None] == jnp.arange(REQUESTS, dtype=jnp.int32)).astype(jnp.float32)
    totals = lax.dot_general(
        members, attribution, (((0,), (0,)), ((), ())), precision=lax.Precision.HIGHEST
    ).reshape(REQUESTS, layers_here, features)
    scored = attribution.astype(jnp.bfloat16).reshape(tokens, layers_here, 1, per_dev, panel)
    spread_out = jnp.sum(
        scored * jnp.swapaxes(named, 0, 1)[..., None], axis=3
    )
    scores = lax.psum_scatter(
        jnp.swapaxes(spread_out, 0, 1), "tok", scatter_dimension=1, tiled=True
    )
    return (scores, totals)


def solution(mesh):
    placed = (
        P("lyr", "tok", None, None),
        P("lyr", "tok", None),
        P("tok"),
        P("tok"),
        P("tok", None),
        P("lyr", "tok", None),
    )
    wide = len({getattr(d, "coords", (0,))[0] for d in mesh.devices.flat})
    grid = (mesh.shape["tok"], mesh.shape["lyr"]) == (16, 2) and wide == 2
    return jax.shard_map(
        functools.partial(per_device, grid=grid),
        mesh=mesh,
        in_specs=placed,
        out_specs=(P("lyr", "tok", None, None), P(None, "lyr", "tok")),
        check_vma=False,
    )
```
